32 devices in a mesh: groups: 2 (over y), ctx: 4 (over z), fsdp: 2 (over x), head: 2 (over core).
Axes of the slice: x: 2, y: 2, z: 4, core: 2. Of those that a mesh axis runs over, the one named last changes fastest.
Arguments:
- tokens: bfloat16 [4096, 3072], P(('groups', 'ctx')), parts along dimension 0, may hold values from -6 to 6
- query_weight: bfloat16 [3072, 4096], P('ctx', ('fsdp', 'head')), may hold values from -0.109375 to 0.109375
- key_weight: bfloat16 [3072, 4096], P('ctx', ('fsdp', 'head')), may hold values from -0.109375 to 0.109375
- value_weight: bfloat16 [3072, 4096], P('ctx', ('fsdp', 'head')), may hold values from -0.109375 to 0.109375
- log_decay: float32 [32, 4096], P(('fsdp', 'head'), ('groups', 'ctx')), parts along dimension 1, may hold values from -1 to 0
Outputs:
- attended: bfloat16 [4096, 4096], P(('groups', 'ctx'), ('fsdp', 'head')), parts along dimension 0
The draws below stay inside these ranges and needn't reach their ends.
There are 2 independent parts, one for each index of `groups`. The reference program is written for one: setup_inputs(seed, part) draws one part's arguments, and reference() takes and returns one part's arrays. A program takes and returns all parts, laid end to end along the dimension named above; an argument that names none is the same for every part. Nothing has to cross between parts.
All inputs are finite; a program needn't handle non-finite values.
Results may differ from the reference program's by a relative error of at most 0.008.
Values may be sent and summed in bfloat16 or wider, within the bound.
No kernel may reach another device: no remote copies, remote signals or barrier semaphores. Data moves between devices by JAX's collectives and lax.ppermute only.
A program may use at most 128 MiB of HBM per device.

```python
import math
import jax
import jax.numpy as jnp
from jax import lax

D = 3072
HEAD_TOTAL = 32
TOK_DEV = 512
SEQUENCE_TOKENS = 2048
HD = 4096


def draw_log_decay(key, part):
    random_subkeys = jax.random.split(key, 7)
    slow_share = 0.5
    slow_heads = jax.random.uniform(random_subkeys[0], (HEAD_TOTAL, 1)) < slow_share
    slow_rate = jnp.exp(jax.random.uniform(random_subkeys[1], (HEAD_TOTAL, 1), minval=math.log(0.2), maxval=math.log(0.8))) / SEQUENCE_TOKENS
    fast_rate = jax.random.uniform(random_subkeys[2], (HEAD_TOTAL, 1), minval=math.log(10.0) / 50.0, maxval=math.log(10.0) / 30.0)
    baseline_decay_rate = jnp.where(slow_heads, slow_rate, fast_rate)
    segment_multiplier = jnp.exp(jax.random.uniform(random_subkeys[3], (HEAD_TOTAL, SEQUENCE_TOKENS // TOK_DEV), minval=math.log(0.7), maxval=math.log(1.4)))
    segment_multiplier = jnp.repeat(segment_multiplier, TOK_DEV, axis=1)
    jitter_multiplier = jax.random.uniform(random_subkeys[4], (HEAD_TOTAL, SEQUENCE_TOKENS), minval=0.6, maxval=1.4)
    spike_locations = jax.random.randint(random_subkeys[5], (2, 1), 0, SEQUENCE_TOKENS)
    token_positions = jnp.arange(SEQUENCE_TOKENS)[None, :]
    spiky_pattern = jnp.any(token_positions == spike_locations, axis=0)[None, :]
    spike_retention = jax.random.uniform(random_subkeys[6], (HEAD_TOTAL, SEQUENCE_TOKENS), minval=0.5, maxval=0.8)
    logarithm_entries = -baseline_decay_rate * segment_multiplier * jitter_multiplier + jnp.where(spiky_pattern, jnp.log(spike_retention), 0.0)
    return logarithm_entries.astype(jnp.float32)


def block_scale(key, extent, pieces, least, top_value):
    level = 1.0
    for axis_at, blocks in pieces:
        draws = jax.random.uniform(jax.random.fold_in(jax.random.fold_in(key, 6), axis_at), (blocks,), jnp.float32, least / len(pieces), top_value / len(pieces))
        level = level * jnp.repeat(jnp.exp(draws), extent[axis_at] // blocks).reshape((-1,) + (1,) * (len(extent) - 1 - axis_at))
    return level


def gaussian(stream_key, shape, deviation, reach, shards=(), dtype=jnp.bfloat16):
    values = jax.random.normal(stream_key, shape, jnp.float32) * deviation
    if len(shards) > 0:
        values = block_scale(stream_key, shape, shards, -0.22, 0.18) * values
    return jnp.clip(values, min=-reach, max=reach).astype(dtype)


def setup_inputs(seed: int = 0, part: int = 0) -> dict:
    splits = jax.random.split(jax.random.key(seed), 6)
    part_keys = jax.random.split(jax.random.fold_in(splits[5], part), 6)
    tokens = gaussian(part_keys[0], (SEQUENCE_TOKENS, D), 1.0, 6.0, ((0, 4),))
    query_weight = gaussian(splits[1], (D, HD), D ** -0.5, 0.109375, ((0, 4), (1, 4)))
    key_weight = gaussian(splits[2], (D, HD), D ** -0.5, 0.109375, ((0, 4), (1, 4)))
    value_weight = gaussian(splits[3], (D, HD), D ** -0.5, 0.109375, ((0, 4), (1, 4)))
    log_decay = draw_log_decay(jax.random.fold_in(jax.random.fold_in(splits[5], part), 71), part)
    return dict(tokens=tokens, query_weight=query_weight, key_weight=key_weight, value_weight=value_weight, log_decay=log_decay)


EPSILON = 1e-06
HIGHEST = lax.Precision.HIGHEST

def reference(tokens, query_weight, key_weight, value_weight, log_decay):
    query_rows = jax.nn.silu(jnp.dot(tokens, query_weight, preferred_element_type=jnp.float32)).astype(jnp.bfloat16)
    key_rows = jax.nn.silu(jnp.dot(tokens, key_weight, preferred_element_type=jnp.float32)).astype(jnp.bfloat16)
    value_rows = jnp.dot(tokens, value_weight, preferred_element_type=jnp.float32).astype(jnp.bfloat16)
    heads_all, row_count = log_decay.shape
    head_size = query_rows.shape[1] // heads_all
    block_rows = math.gcd(row_count, 512)
    block_count = row_count // block_rows

    def into_blocks(matrix):
        return matrix.reshape(block_count, block_rows, heads_all, head_size).astype(jnp.float32)
    cumulative_all = jnp.cumsum(log_decay, axis=1)
    starts = jnp.concatenate([jnp.zeros((heads_all, 1), jnp.float32), cumulative_all[:, :-1]], axis=1)
    cum_blocks = cumulative_all.reshape(heads_all, block_count, block_rows).transpose(1, 0, 2)
    start_blocks = starts.reshape(heads_all, block_count, block_rows).transpose(1, 0, 2)[:, :, 0]
    causal = jnp.arange(block_rows)[None, :] <= jnp.arange(block_rows)[:, None]

    def advance(carry_state, inputs):
        queries, keyset, valueset, cumulative, block_start = inputs
        scores = jnp.einsum('qhd,khd->hqk', queries, keyset, precision=HIGHEST)
        decay_gaps = jnp.where(causal[None], cumulative[:, :, None] - cumulative[:, None, :], -jnp.inf)
        weights = (scores * jnp.exp(decay_gaps)).astype(jnp.bfloat16).astype(jnp.float32)
        within_part = jnp.einsum('hqk,khe->qhe', weights, valueset, precision=HIGHEST)
        state_bf = carry_state.astype(jnp.bfloat16).astype(jnp.float32)
        carried_part = jnp.einsum('qhd,hde->qhe', queries, state_bf, precision=HIGHEST) * jnp.exp(cumulative - block_start[:, None]).T[:, :, None]
        raw_out = within_part + carried_part
        to_end = jnp.exp(cumulative[:, -1:] - cumulative)
        scaled = (keyset * to_end.T[:, :, None]).astype(jnp.bfloat16).astype(jnp.float32)
        fresh_state = jnp.einsum('khd,khe->hde', scaled, valueset, precision=HIGHEST)
        carry_state = jnp.exp(cumulative[:, -1] - block_start)[:, None, None] * carry_state + fresh_state
        inverse_rms = lax.rsqrt(lax.optimization_barrier(jnp.mean(raw_out * raw_out, axis=-1, keepdims=True)) + EPSILON)
        return (carry_state, (raw_out * inverse_rms).astype(jnp.bfloat16))
    initial = jnp.zeros((heads_all, head_size, head_size), jnp.float32)
    final_state, outputs = lax.scan(advance, initial, (into_blocks(query_rows), into_blocks(key_rows), into_blocks(value_rows), cum_blocks, start_blocks))
    return outputs.reshape(row_count, heads_all * head_size)
```

```python
import functools
import jax
import jax.numpy as jnp
from jax import lax
from jax.experimental import pallas as pl
from jax.experimental.pallas import tpu as pltpu
from jax.sharding import PartitionSpec as P

EPSILON = 1e-06


def prefix(shard, axis, join, neutral):
    place = lax.axis_index(axis)
    gathered = jax.tree.map(
        lambda a, kind: lax.all_gather(a.astype(kind), axis), shard, (jnp.bfloat16, jnp.bfloat16)
    )
    state = jax.tree.map(lambda a, e: jnp.zeros_like(a) + jnp.asarray(e, a.dtype), shard, neutral)

    def one(turn, state):
        return join(
            state,
            jax.tree.map(
                lambda a, own: lax.dynamic_index_in_dim(a, turn, 0, False).astype(own.dtype),
                gathered,
                shard,
            ),
        )

    return lax.fori_loop(0, place, one, state)


def row_folder(tokens):

    def accumulate(running, portions, offset):
        return tuple(
            (jnp.dot(tokens, portion, preferred_element_type=jnp.float32) for portion in portions)
        )

    return accumulate


def combine_states(earlier, later):
    return (earlier[0] + later[0], jnp.exp(later[0])[:, None, None] * earlier[1] + later[1])


def local_summary(key_rows, value_rows, cumulative):
    heads_here, row_count = cumulative.shape
    head_size = key_rows.shape[1] // heads_here
    to_end = jnp.exp(cumulative[:, -1:] - cumulative)
    scaled = (
        key_rows.reshape(row_count, heads_here, head_size).astype(jnp.float32)
        * to_end.T[:, :, None]
    ).astype(jnp.bfloat16)
    valueset = value_rows.reshape(row_count, heads_here, head_size)
    return jnp.einsum("khd,khe->hde", scaled, valueset, preferred_element_type=jnp.float32)


def carried(total_decay, own_state):
    identity = (jnp.zeros_like(total_decay), jnp.zeros_like(own_state))
    return prefix((total_decay, own_state), "ctx", combine_states, identity)


def attend(query_rows, key_rows, value_rows, cumulative, incoming):
    heads_here, row_count = cumulative.shape
    head_size = query_rows.shape[1] // heads_here
    block_rows = min(row_count, 512)
    queries = query_rows.reshape(row_count, heads_here, head_size)
    keyset = key_rows.reshape(row_count, heads_here, head_size)
    valueset = value_rows.reshape(row_count, heads_here, head_size)
    incoming_bf = incoming.astype(jnp.bfloat16)
    key_index = jnp.arange(row_count)

    def one_block(block_index):
        first_row = block_index * block_rows
        query_index = first_row + jnp.arange(block_rows)
        scores = jnp.einsum("qhd,khd->hqk", queries, keyset, preferred_element_type=jnp.float32)
        causal = key_index[None, :] <= query_index[:, None]
        decay_gaps = jnp.where(
            causal[None], cumulative[:, :, None] - cumulative[:, None, :], -jnp.inf
        )
        weights = (scores * jnp.exp(decay_gaps)).astype(jnp.bfloat16)
        within_part = jnp.einsum(
            "hqk,khe->qhe", weights, valueset, preferred_element_type=jnp.float32
        )
        carried_part = (
            jnp.einsum("qhd,hde->qhe", queries, incoming_bf, preferred_element_type=jnp.float32)
            * jnp.exp(cumulative).T[:, :, None]
        )
        raw_out = within_part + carried_part
        inverse_rms = lax.rsqrt(jnp.mean(raw_out * raw_out, axis=-1, keepdims=True) + EPSILON)
        return (raw_out * inverse_rms).astype(jnp.bfloat16)

    blocks = lax.map(one_block, jnp.arange(row_count // block_rows))
    return blocks.reshape(row_count, heads_here * head_size)


def body(tokens, query_weight, key_weight, value_weight, log_decay):
    row_count = tokens.shape[0]
    zero_rows = jnp.zeros((row_count, query_weight.shape[1]), jnp.float32)
    accumulate = row_folder(tokens)
    cumulative = jnp.cumsum(log_decay, axis=1)
    total_decay = cumulative[:, -1]
    query_sum, key_sum, value_sum = accumulate(
        (zero_rows, zero_rows, zero_rows),
        (
            lax.all_gather(query_weight, "ctx", axis=0, tiled=True),
            lax.all_gather(key_weight, "ctx", axis=0, tiled=True),
            lax.all_gather(value_weight, "ctx", axis=0, tiled=True),
        ),
        jnp.int32(0),
    )
    query_rows = jax.nn.silu(query_sum).astype(jnp.bfloat16)
    key_rows = jax.nn.silu(key_sum).astype(jnp.bfloat16)
    value_rows = value_sum.astype(jnp.bfloat16)
    incoming = carried(total_decay, local_summary(key_rows, value_rows, cumulative))[1]
    return attend(query_rows, key_rows, value_rows, cumulative, incoming)


SIDES = ("own", "ctx", "groups", "both")


def xor_permute(array, mesh, axis, flip):
    return lax.ppermute(array, axis, [(at, at ^ flip) for at in range(mesh.shape[axis])])


def after(array, *earlier):
    return lax.optimization_barrier((array, *earlier))[0]


def silu(rows):
    return rows / (1.0 + jnp.exp(-rows))


def project(places, token_refs, weight_refs, accumulators, step):
    for flip in range(len(weight_refs)):

        @pl.when(step == flip)
        def _(flip=flip):
            weight = jnp.concatenate(
                [
                    jnp.concatenate([half[...] for half in halves], axis=0)
                    for halves in weight_refs[flip]
                ],
                axis=1,
            )
            for token_ref, accumulator in zip(token_refs, accumulators):
                product = jnp.dot(token_ref[...], weight, preferred_element_type=jnp.float32)
                if flip == 0:
                    accumulator[...] = product
                else:
                    accumulator[...] += product


def column_of(row, width):
    return jnp.transpose(jnp.broadcast_to(row, (width, row.shape[1])))


def key_value_kernel(heads, size, parts, places, *refs):
    sides = len(SIDES)
    token_refs, refs = refs[:sides], refs[sides:]
    decay_refs, refs = refs[:sides], refs[sides:]
    flips = parts[0]
    count = flips * 2 * heads * 2
    flat, refs = refs[:count], refs[count:]
    weight_refs = [
        [[flat[(flip * 2 * heads + block) * 2 + half] for half in range(2)] for block in range(2 * heads)]
        for flip in range(flips)
    ]
    key_refs, refs = refs[:sides], refs[sides:]
    value_refs, refs = refs[:sides], refs[sides:]
    state_ref, refs = refs[0], refs[1:]
    accumulators = refs
    step = pl.program_id(0)
    project(places, token_refs, weight_refs, accumulators, step)

    @pl.when(step == flips - 1)
    def _():
        for side in range(sides):
            for head in range(heads):
                at = 2 * head * size
                key = silu(accumulators[side][:, at : at + size]).astype(jnp.bfloat16)
                value = accumulators[side][:, at + size : at + 2 * size].astype(jnp.bfloat16)
                row = decay_refs[side][head : head + 1, :]
                column = column_of(row, size)
                to_end = jnp.exp(column[-1:, :] - column)
                scaled = (key.astype(jnp.float32) * to_end).astype(jnp.bfloat16)
                state_ref[head, side] = lax.dot_general(
                    scaled, value, (((0,), (0,)), ((), ())), preferred_element_type=jnp.float32
                )
                key_refs[side][:, head * size : (head + 1) * size] = key
                value_refs[side][:, head * size : (head + 1) * size] = value


def query_kernel(heads, size, parts, places, *refs):
    sides = len(SIDES)
    token_refs, refs = refs[:sides], refs[sides:]
    decay_refs, refs = refs[:sides], refs[sides:]
    flips, head = parts
    count = flips * 2
    flat, refs = refs[:count], refs[count:]
    weight_refs = [[[flat[flip * 2 + half] for half in range(2)]] for flip in range(flips)]
    key_refs, refs = refs[:sides], refs[sides:]
    value_refs, refs = refs[:sides], refs[sides:]
    incoming_ref, refs = refs[0], refs[1:]
    out_refs, accumulators = refs[:sides], refs[sides:]
    step = pl.program_id(0)
    project(places, token_refs, weight_refs, accumulators, step)

    @pl.when(step == flips - 1)
    def _():
        rows = token_refs[0].shape[0]
        causal = lax.broadcasted_iota(jnp.int32, (rows, rows), 1) <= lax.broadcasted_iota(
            jnp.int32, (rows, rows), 0
        )
        for side in range(sides):
            query = silu(accumulators[side][...]).astype(jnp.bfloat16)
            key, value = key_refs[side][...], value_refs[side][...]
            row = decay_refs[side][head : head + 1, :]
            column = column_of(row, size)
            wide = jnp.concatenate([column] * (rows // size), axis=1)
            scores = lax.dot_general(
                query, key, (((1,), (1,)), ((), ())), preferred_element_type=jnp.float32
            )
            weights = (scores * jnp.exp(jnp.where(causal, wide - row, -jnp.inf))).astype(jnp.bfloat16)
            raw = jnp.dot(weights, value, preferred_element_type=jnp.float32)
            raw += jnp.exp(column) * jnp.dot(
                query, incoming_ref[side], preferred_element_type=jnp.float32
            )
            scale = lax.rsqrt(jnp.mean(raw * raw, axis=1, keepdims=True) + EPSILON)
            out_refs[side][...] = (raw * scale).astype(jnp.bfloat16)


def merge_kernel(heads, size, place, *refs):
    pieces, out_ref = refs[:-1], refs[-1]
    for side in range(len(SIDES)):
        for head in range(heads):
            at = pl.multiple_of(((place[0] ^ side) * heads + head) * size, size)
            out_ref[:, pl.ds(at, size)] = pieces[side * heads + head][...]


def whole(shape):
    return pl.BlockSpec(shape, lambda step, places: (0,) * len(shape))


def spread_body(mesh, tokens, query_weight, key_weight, value_weight, log_decay):
    rows, width = tokens.shape
    depth = query_weight.shape[0]
    heads_here = log_decay.shape[0]
    size = query_weight.shape[1] // heads_here
    flips = mesh.shape["ctx"]
    shares = mesh.shape["fsdp"] * mesh.shape["head"]
    heads = heads_here // 4
    group, turn = lax.axis_index("groups"), lax.axis_index("ctx")
    share = lax.axis_index("fsdp") * 2 + lax.axis_index("head")
    mine = group * 2 + turn % 2
    half_rows = depth // 2

    blocks = [(weight, head) for head in range(heads) for weight in (key_weight, value_weight)]
    blocks += [(query_weight, head) for head in range(heads)]

    def stacked(owner, first, last):
        cut = []
        for half in range(first, last):
            weight, head = blocks[half // 2]
            cut.append(
                lax.dynamic_slice(
                    weight,
                    ((half % 2) * half_rows, (owner * heads + head) * size),
                    (half_rows, size),
                )
            )
        return jnp.concatenate(cut, axis=0)

    bounds = [0] + list(range(1, 2 * len(blocks), 2)) + [2 * len(blocks)]
    chunks = []
    for number, (first, last) in enumerate(zip(bounds[:-1], bounds[1:])):
        kept, sent = stacked(mine, first, last), stacked(mine ^ 1, first, last)
        if number >= 2:
            kept, sent = lax.optimization_barrier((kept, sent, *chunks[number - 2][1:]))[:2]
        chunks.append(
            [kept] + [xor_permute(sent if flip % 2 else kept, mesh, "ctx", flip) for flip in range(1, flips)]
        )

    quarter_width = width // shares

    def quarter(at):
        return lax.dynamic_slice(tokens, (0, at * quarter_width), (rows, quarter_width))

    def over_cores(first, second):
        return jnp.concatenate(
            [first, xor_permute(first, mesh, "head", 1), second, xor_permute(second, mesh, "head", 1)],
            axis=1,
        )

    from_ctx = xor_permute(quarter(share), mesh, "ctx", 1)
    from_groups = [xor_permute(quarter(share ^ flip), mesh, "groups", 1) for flip in (0, 2)]
    from_both = xor_permute(from_ctx, mesh, "groups", 1)
    token_sets = [
        tokens,
        over_cores(from_ctx, xor_permute(from_ctx, mesh, "fsdp", 1)),
        over_cores(*from_groups),
        over_cores(from_both, xor_permute(from_both, mesh, "fsdp", 1)),
    ]
    places = jnp.stack([turn, turn ^ share]).astype(jnp.int32)

    cumulative = jnp.cumsum(log_decay, axis=1)
    ctx_decay = xor_permute(cumulative, mesh, "ctx", 1)
    decays = [
        lax.dynamic_slice(array, (mine * heads, 0), (heads, rows))
        for array in (
            cumulative,
            ctx_decay,
            xor_permute(cumulative, mesh, "groups", 1),
            xor_permute(ctx_decay, mesh, "groups", 1),
        )
    ]

    def token_spec(side):
        kind = 0 if side == 0 else 1
        return pl.BlockSpec((rows, depth), lambda step, places: (0, places[kind] ^ step))

    def weight_operands(wanted):
        arrays, specs = [], []
        for flip in range(flips):
            for block in wanted:
                for half in (2 * block, 2 * block + 1):
                    number = (half + 1) // 2
                    offset = half - bounds[number]
                    arrays.append(chunks[number][flip])
                    specs.append(
                        pl.BlockSpec((half_rows, size), lambda step, places, offset=offset: (offset, 0))
                    )
        return arrays, specs

    sides = len(SIDES)
    token_specs = [token_spec(side) for side in range(sides)]
    decay_specs = [whole((heads, rows))] * sides
    params = pltpu.CompilerParams(vmem_limit_bytes=56 * 1024 * 1024)
    arrays, specs = weight_operands(range(2 * heads))
    results = pl.pallas_call(
        functools.partial(key_value_kernel, heads, size, (flips,)),
        grid_spec=pltpu.PrefetchScalarGridSpec(
            num_scalar_prefetch=1,
            grid=(flips,),
            in_specs=token_specs + decay_specs + specs,
            out_specs=[whole((rows, heads * size))] * (2 * sides) + [whole((heads, sides, size, size))],
            scratch_shapes=[pltpu.VMEM((rows, 2 * heads * size), jnp.float32)] * sides,
        ),
        out_shape=[jax.ShapeDtypeStruct((rows, heads * size), jnp.bfloat16)] * (2 * sides)
        + [jax.ShapeDtypeStruct((heads, sides, size, size), jnp.float32)],
        compiler_params=params,
        cost_estimate=pl.CostEstimate(
            flops=2 * sides * rows * width * 2 * heads * size,
            bytes_accessed=2 * (sides * rows * width + width * 2 * heads * size),
            transcendentals=sides * rows * 2 * heads * size,
        ),
        name="key_value",
    )(places, *token_sets, *decays, *arrays)
    keys, values, states = results[:sides], results[sides : 2 * sides], results[2 * sides]

    totals = jnp.stack([decay[:, -1] for decay in decays], axis=1)
    fresh = states.reshape(heads, 2, 2, size, size)
    total = totals.reshape(heads, 2, 2)
    fade = jnp.exp(total)[..., None, None]
    odd = turn % 2 == 1
    first_fresh = jnp.where(odd, fresh[:, :, 1], fresh[:, :, 0])
    last_fresh = jnp.where(odd, fresh[:, :, 0], fresh[:, :, 1])
    first_fade = jnp.where(odd, fade[:, :, 1], fade[:, :, 0])
    last_fade = jnp.where(odd, fade[:, :, 0], fade[:, :, 1])
    pair_state = (last_fade * first_fresh + last_fresh).astype(jnp.bfloat16)
    before = lax.ppermute(pair_state, "ctx", [(0, 2), (1, 3)]).astype(jnp.float32)
    between = first_fade * before + first_fresh
    incoming = jnp.stack(
        [jnp.where(odd, between, before), jnp.where(odd, before, between)], axis=2
    ).reshape(heads, sides, size, size).astype(jnp.bfloat16)

    pieces = [[] for _ in SIDES]
    both = [
        (at, (at // flips ^ 1) * flips + (at % flips ^ 1)) for at in range(mesh.shape["groups"] * flips)
    ]
    for head in range(heads):
        arrays, specs = weight_operands([2 * heads + head])
        head_spec = pl.BlockSpec((rows, size), lambda step, places, head=head: (0, head))
        attended = pl.pallas_call(
            functools.partial(query_kernel, heads, size, (flips, head)),
            grid_spec=pltpu.PrefetchScalarGridSpec(
                num_scalar_prefetch=1,
                grid=(flips,),
                in_specs=token_specs
                + decay_specs
                + specs
                + [head_spec] * (2 * sides)
                + [whole((sides, size, size))],
                out_specs=[whole((rows, size))] * sides,
                scratch_shapes=[pltpu.VMEM((rows, size), jnp.float32)] * sides,
            ),
            out_shape=[jax.ShapeDtypeStruct((rows, size), jnp.bfloat16)] * sides,
            compiler_params=params,
            cost_estimate=pl.CostEstimate(
                flops=2 * sides * rows * size * (width + 2 * rows + size),
                bytes_accessed=2 * (sides * rows * width + width * size),
                transcendentals=sides * rows * (rows + 2 * size),
            ),
            name="query",
        )(places, *token_sets, *decays, *arrays, *keys, *values, incoming[head])
        pieces[0].append(attended[0])
        pieces[1].append(xor_permute(attended[1], mesh, "ctx", 1))
        pieces[2].append(xor_permute(attended[2], mesh, "groups", 1))
        pieces[3].append(lax.ppermute(attended[3], ("groups", "ctx"), both))

    flat = [piece for side in pieces for piece in side]
    return pl.pallas_call(
        functools.partial(merge_kernel, heads, size),
        grid_spec=pltpu.PrefetchScalarGridSpec(
            num_scalar_prefetch=1,
            grid=(1,),
            in_specs=[whole((rows, size))] * len(flat),
            out_specs=whole((rows, heads_here * size)),
        ),
        out_shape=jax.ShapeDtypeStruct((rows, heads_here * size), jnp.bfloat16),
        name="merge",
    )(mine[None].astype(jnp.int32), *flat)


def spreads(mesh, tokens, query_weight, key_weight, value_weight, log_decay):
    sizes = tuple(mesh.shape[axis] for axis in ("groups", "ctx", "fsdp", "head"))
    if sizes != (2, 4, 2, 2):
        return False
    heads_here = log_decay.shape[0]
    depth = query_weight.shape[0]
    size = query_weight.shape[1] // heads_here
    return (
        heads_here % 4 == 0
        and size == 128
        and depth % 256 == 0
        and depth * 4 == tokens.shape[1]
        and tokens.shape[0] % 128 == 0
        and tokens.shape[0] <= 512
    )


def local_body(mesh, *arrays):
    if spreads(mesh, *arrays):
        return spread_body(mesh, *arrays)
    return body(*arrays)


def solution(mesh):
    return jax.shard_map(
        functools.partial(local_body, mesh),
        mesh=mesh,
        in_specs=(
            P(("groups", "ctx"), None),
            P("ctx", ("fsdp", "head")),
            P("ctx", ("fsdp", "head")),
            P("ctx", ("fsdp", "head")),
            P(("fsdp", "head"), ("groups", "ctx")),
        ),
        out_specs=P(("groups", "ctx"), ("fsdp", "head")),
        check_vma=False,
    )
```

```python
import functools
import jax
import jax.numpy as jnp
from jax import lax
from jax.experimental import pallas as pl
from jax.experimental.pallas import tpu as pltpu
from jax.sharding import PartitionSpec as P

EPSILON = 1e-06


def prefix(shard, axis, join, neutral):
    place = lax.axis_index(axis)
    gathered = jax.tree.map(
        lambda a, kind: lax.all_gather(a.astype(kind), axis), shard, (jnp.bfloat16, jnp.bfloat16)
    )
    state = jax.tree.map(lambda a, e: jnp.zeros_like(a) + jnp.asarray(e, a.dtype), shard, neutral)

    def one(turn, state):
        return join(
            state,
            jax.tree.map(
                lambda a, own: lax.dynamic_index_in_dim(a, turn, 0, False).astype(own.dtype),
                gathered,
                shard,
            ),
        )

    return lax.fori_loop(0, place, one, state)


def row_folder(tokens):

    def accumulate(running, portions, offset):
        return tuple(
            (jnp.dot(tokens, portion, preferred_element_type=jnp.float32) for portion in portions)
        )

    return accumulate


def combine_states(earlier, later):
    return (earlier[0] + later[0], jnp.exp(later[0])[:, None, None] * earlier[1] + later[1])


def local_summary(key_rows, value_rows, cumulative):
    heads_here, row_count = cumulative.shape
    head_size = key_rows.shape[1] // heads_here
    to_end = jnp.exp(cumulative[:, -1:] - cumulative)
    scaled = (
        key_rows.reshape(row_count, heads_here, head_size).astype(jnp.float32)
        * to_end.T[:, :, None]
    ).astype(jnp.bfloat16)
    valueset = value_rows.reshape(row_count, heads_here, head_size)
    return jnp.einsum("khd,khe->hde", scaled, valueset, preferred_element_type=jnp.float32)


def carried(total_decay, own_state):
    identity = (jnp.zeros_like(total_decay), jnp.zeros_like(own_state))
    return prefix((total_decay, own_state), "ctx", combine_states, identity)


def attend(query_rows, key_rows, value_rows, cumulative, incoming):
    heads_here, row_count = cumulative.shape
    head_size = query_rows.shape[1] // heads_here
    block_rows = min(row_count, 512)
    queries = query_rows.reshape(row_count, heads_here, head_size)
    keyset = key_rows.reshape(row_count, heads_here, head_size)
    valueset = value_rows.reshape(row_count, heads_here, head_size)
    incoming_bf = incoming.astype(jnp.bfloat16)
    key_index = jnp.arange(row_count)

    def one_block(block_index):
        first_row = block_index * block_rows
        query_index = first_row + jnp.arange(block_rows)
        scores = jnp.einsum("qhd,khd->hqk", queries, keyset, preferred_element_type=jnp.float32)
        causal = key_index[None, :] <= query_index[:, None]
        decay_gaps = jnp.where(
            causal[None], cumulative[:, :, None] - cumulative[:, None, :], -jnp.inf
        )
        weights = (scores * jnp.exp(decay_gaps)).astype(jnp.bfloat16)
        within_part = jnp.einsum(
            "hqk,khe->qhe", weights, valueset, preferred_element_type=jnp.float32
        )
        carried_part = (
            jnp.einsum("qhd,hde->qhe", queries, incoming_bf, preferred_element_type=jnp.float32)
            * jnp.exp(cumulative).T[:, :, None]
        )
        raw_out = within_part + carried_part
        inverse_rms = lax.rsqrt(jnp.mean(raw_out * raw_out, axis=-1, keepdims=True) + EPSILON)
        return (raw_out * inverse_rms).astype(jnp.bfloat16)

    blocks = lax.map(one_block, jnp.arange(row_count // block_rows))
    return blocks.reshape(row_count, heads_here * head_size)


def body(tokens, query_weight, key_weight, value_weight, log_decay):
    row_count = tokens.shape[0]
    zero_rows = jnp.zeros((row_count, query_weight.shape[1]), jnp.float32)
    accumulate = row_folder(tokens)
    cumulative = jnp.cumsum(log_decay, axis=1)
    total_decay = cumulative[:, -1]
    query_sum, key_sum, value_sum = accumulate(
        (zero_rows, zero_rows, zero_rows),
        (
            lax.all_gather(query_weight, "ctx", axis=0, tiled=True),
            lax.all_gather(key_weight, "ctx", axis=0, tiled=True),
            lax.all_gather(value_weight, "ctx", axis=0, tiled=True),
        ),
        jnp.int32(0),
    )
    query_rows = jax.nn.silu(query_sum).astype(jnp.bfloat16)
    key_rows = jax.nn.silu(key_sum).astype(jnp.bfloat16)
    value_rows = value_sum.astype(jnp.bfloat16)
    incoming = carried(total_decay, local_summary(key_rows, value_rows, cumulative))[1]
    return attend(query_rows, key_rows, value_rows, cumulative, incoming)


SIDES = ("own", "ctx", "groups", "both")
PIECE = 128
ANY = pl.BlockSpec(memory_space=pl.ANY)
VMEM = pl.BlockSpec(memory_space=pltpu.VMEM)
SCALARS = pl.BlockSpec(memory_space=pltpu.SMEM)


def xor_permute(array, mesh, axis, flip):
    return lax.ppermute(array, axis, [(at, at ^ flip) for at in range(mesh.shape[axis])])


def after(arrays, *earlier):
    return lax.optimization_barrier((*arrays, *earlier))[: len(arrays)]


def in_three(array):
    parts = []
    for _ in range(3):
        part = lax.reduce_precision(array, 8, 7)
        parts.append(part.astype(jnp.bfloat16))
        array = array - part
    return jnp.concatenate(parts, axis=0)


def silu(rows):
    return rows / (1.0 + jnp.exp(-rows))


def running_sum(rows):
    lane = lax.broadcasted_iota(jnp.int32, rows.shape, 1)
    shift = 1
    while shift < rows.shape[1]:
        rows += jnp.where(lane >= shift, pltpu.roll(rows, shift, 1), 0.0)
        shift *= 2
    return rows


def column_of(row):
    return jnp.transpose(jnp.broadcast_to(row, (PIECE, row.shape[1])))


def token_copies(places, token_refs, held, semaphores):
    turn, share = places[0], places[1] * 2 + places[2]
    own_ref, quarter_refs = token_refs[0], token_refs[1:]
    width = held.shape[3]

    def copy(source, side, flip):
        return pltpu.make_async_copy(source, held.at[side, flip], semaphores.at[side, flip])

    def start():
        for side in range(len(SIDES)):
            for flip in range(held.shape[1]):
                block = turn ^ flip
                if side == 0:
                    at = pl.multiple_of(block * width, width)
                    copy(own_ref.at[:, pl.ds(at, width)], side, flip).start()
                    continue
                for place, ref in enumerate(quarter_refs[4 * (side - 1) : 4 * side]):

                    @pl.when(block ^ share == place)
                    def _(ref=ref):
                        copy(ref.at[0 : held.shape[2], :], side, flip).start()

    def wait(side):
        for flip in range(held.shape[1]):
            copy(quarter_refs[0].at[0 : held.shape[2], :], side, flip).wait()

    return start, wait


def project(token_refs, weights):
    total = None
    for token_ref, weight in zip(token_refs, weights):
        product = jnp.dot(token_ref[...], weight, preferred_element_type=jnp.float32)
        total = product if total is None else total + product
    return total


def piece_rows(rows):
    return [slice(at, at + PIECE) for at in range(0, rows, PIECE)]


def key_value_kernel(heads, size, flips, places, *refs):
    sides = len(SIDES)
    token_refs, refs = refs[:13], refs[13:]
    decay_refs, refs = refs[:sides], refs[sides:]
    source_ref, held, key_ref, value_ref, state_ref, sum_ref, fade_ref, mask_ref, pair_ref = refs[:9]
    weight_ref, decay_ref, semaphores, weight_semaphores = refs[9:]
    loads = [
        pltpu.make_async_copy(
            source_ref.at[places[0] ^ flip], weight_ref.at[flip], weight_semaphores.at[flip]
        )
        for flip in range(flips)
    ]
    for load in loads:
        load.start()
    start, wait = token_copies(places, token_refs, held, semaphores)
    start()
    odd = places[0] % 2 == 1
    causal = lax.broadcasted_iota(jnp.int32, (PIECE, PIECE), 1) <= lax.broadcasted_iota(
        jnp.int32, (PIECE, PIECE), 0
    )
    cuts = piece_rows(key_ref.shape[1])
    for side in range(sides):
        part = decay_refs[side][...].astype(jnp.float32)
        count = part.shape[0] // 3
        log_decay = part[:count] + (part[count : 2 * count] + part[2 * count :])
        decay_ref[...] = running_sum(log_decay[:, : sum_ref.shape[2]])
        for head in range(heads):
            sum_ref[side, head : head + 1, :] = decay_ref[pl.ds(places[3] * heads + head, 1), :]
    for load in loads:
        load.wait()
    for side in range(sides):
        wait(side)
        for head in range(heads):
            at = slice(2 * head * size, 2 * (head + 1) * size)
            both = project(
                [held.at[side, flip] for flip in range(flips)],
                [weight_ref[flip, :, at] for flip in range(flips)],
            )
            key = silu(both[:, :size])
            key_bf = key.astype(jnp.bfloat16)
            key = key_bf.astype(jnp.float32)
            value = both[:, size:].astype(jnp.bfloat16)
            key_ref[side, :, head * size : (head + 1) * size] = key_bf
            value_ref[side, :, head * size : (head + 1) * size] = value
            row = sum_ref[side, head : head + 1, :]
            column = column_of(row)
            ends = [column[cut.stop - 1 : cut.stop, :] for cut in cuts]
            fresh = []
            for cut, end in zip(cuts, ends):
                scaled = (key[cut] * jnp.exp(end - column[cut])).astype(jnp.bfloat16)
                fresh.append(
                    lax.dot_general(
                        scaled, value[cut], (((0,), (0,)), ((), ())), preferred_element_type=jnp.float32
                    )
                )
            state = fresh[0]
            for piece, cut in enumerate(cuts):
                begin = ends[piece - 1] if piece else jnp.zeros_like(ends[0])
                if piece:
                    state = jnp.exp(ends[piece] - begin) * state + fresh[piece]
                state_ref[head, side, piece] = state
                fade_ref[head, side, cut, :] = jnp.exp(column[cut] - begin)
                gaps = jnp.where(causal, column[cut] - row[:, cut], -jnp.inf)
                mask_ref[head, side, cut, :] = jnp.exp(gaps)
    last = len(cuts) - 1
    end = sum_ref.shape[2] - 1
    for head in range(heads):
        for pair in range(2):
            own, other = state_ref[head, 2 * pair, last], state_ref[head, 2 * pair + 1, last]
            own_total = sum_ref[2 * pair, head : head + 1, end:]
            other_total = sum_ref[2 * pair + 1, head : head + 1, end:]
            total = jnp.where(odd, own_total, other_total)
            first, second = jnp.where(odd, other, own), jnp.where(odd, own, other)
            pair_ref[head, pair] = (jnp.exp(total) * first + second).astype(jnp.bfloat16)


def query_kernel(head, columns, flips, places, *refs):
    sides = len(SIDES)
    held, refs = refs[0], refs[1:]
    weight_refs, refs = refs[:flips], refs[flips:]
    key_ref, value_ref, state_ref, sum_ref, fade_ref, mask_ref, before_ref = refs[:7]
    out_refs = refs[7:]
    odd = places[0] % 2 == 1
    cuts = piece_rows(key_ref.shape[1])
    last = len(cuts) - 1
    end = sum_ref.shape[2] - 1
    for side in range(sides):
        partner = side ^ 1
        before = before_ref[head, side // 2].astype(jnp.float32)
        total = sum_ref[partner, head : head + 1, end:]
        later = jnp.exp(total) * before + state_ref[head, partner, last]
        second = odd if side % 2 == 0 else jnp.logical_not(odd)
        incoming = jnp.where(second, later, before)
        states = [incoming.astype(jnp.bfloat16)]
        for piece in range(1, len(cuts)):
            stop = cuts[piece].start - 1
            sofar = jnp.exp(sum_ref[side, head : head + 1, stop : stop + 1])
            states.append((state_ref[head, side, piece - 1] + sofar * incoming).astype(jnp.bfloat16))
        query = project(
            [held.at[side, flip] for flip in range(flips)],
            [ref[:, columns] if flip == 1 else ref[...] for flip, ref in enumerate(weight_refs)],
        )
        query = silu(query).astype(jnp.bfloat16)
        at = slice(head * PIECE, (head + 1) * PIECE)
        weights = [
            (
                lax.dot_general(
                    query[cut],
                    key_ref[side, cut, at],
                    (((1,), (1,)), ((), ())),
                    preferred_element_type=jnp.float32,
                )
                * mask_ref[head, side, cut, :]
            ).astype(jnp.bfloat16)
            for cut in cuts
        ]
        raws = [
            jnp.dot(query[cut], state, preferred_element_type=jnp.float32) * fade_ref[head, side, cut, :]
            for cut, state in zip(cuts, states)
        ]
        raws = [
            raw + jnp.dot(weight, value_ref[side, cut, at], preferred_element_type=jnp.float32)
            for raw, weight, cut in zip(raws, weights, cuts)
        ]
        for raw, cut in zip(raws, cuts):
            scale = lax.rsqrt(jnp.mean(raw * raw, axis=1, keepdims=True) + EPSILON)
            out_refs[side][cut, :] = (raw * scale).astype(jnp.bfloat16)


def merge_kernel(heads, size, places, *refs):
    pieces, out_ref = refs[:-1], refs[-1]
    for side in range(len(SIDES)):
        for head in range(heads):
            at = pl.multiple_of(((places[3] ^ side) * heads + head) * size, size)
            out_ref[:, pl.ds(at, size)] = pieces[side * heads + head][...]


def pack_kernel(heads, size, places, key_ref, value_ref, out_ref):
    for head in range(heads):
        at, to = head * size, 2 * head * size
        out_ref[0, :, to : to + size] = key_ref[:, at : at + size]
        out_ref[0, :, to + size : to + 2 * size] = value_ref[:, at : at + size]


def spread_body(mesh, tokens, query_weight, key_weight, value_weight, log_decay):
    rows, width = tokens.shape
    depth = query_weight.shape[0]
    heads_here = log_decay.shape[0]
    size = query_weight.shape[1] // heads_here
    flips = mesh.shape["ctx"]
    heads = heads_here // 4
    sides = len(SIDES)
    group, turn = lax.axis_index("groups"), lax.axis_index("ctx")
    plane, core = lax.axis_index("fsdp"), lax.axis_index("head")
    mine = group * 2 + turn % 2
    places = jnp.stack([turn, core, plane, mine]).astype(jnp.int32)
    both = [
        (at, (at // flips ^ 1) * flips + (at % flips ^ 1)) for at in range(mesh.shape["groups"] * flips)
    ]

    share = core * 2 + plane
    quarter = lax.dynamic_slice(tokens, (0, share * depth), (rows, depth))
    tail = jnp.pad(in_three(log_decay), ((0, 0), (0, depth - rows)))
    quarter = jnp.concatenate([quarter, tail], axis=0)
    beside = lax.dynamic_slice(tokens, (0, (share ^ 1) * depth), (rows, depth))

    block = (depth, heads * size)
    packed_shape = (flips, depth, 2 * heads * size)
    owner = pl.BlockSpec(block, lambda step, places: (0, places[3] ^ ((places[0] ^ step) % 2)))
    packed = pl.pallas_call(
        functools.partial(pack_kernel, heads, size),
        grid_spec=pltpu.PrefetchScalarGridSpec(
            num_scalar_prefetch=1,
            grid=(flips,),
            in_specs=[owner, owner],
            out_specs=pl.BlockSpec((1,) + packed_shape[1:], lambda step, places: (step, 0, 0)),
        ),
        out_shape=jax.ShapeDtypeStruct(packed_shape, jnp.bfloat16),
        cost_estimate=pl.CostEstimate(flops=0, bytes_accessed=32 * depth * heads * size, transcendentals=0),
        name="pack",
    )(places, key_weight, value_weight)

    key_value = lax.all_to_all(packed, "ctx", 0, 0)

    from_ctx = xor_permute(quarter, mesh, "ctx", 1)
    ctx_core = xor_permute(from_ctx, mesh, "head", 1)
    (from_ctx,) = after((from_ctx,), ctx_core)
    from_groups = xor_permute(quarter, mesh, "groups", 1)
    ctx_plane = xor_permute(from_ctx, mesh, "fsdp", 1)
    from_both = xor_permute(from_ctx, mesh, "groups", 1)
    groups_plane = xor_permute(after((beside,), from_ctx)[0], mesh, "groups", 1)
    both_core = xor_permute(from_both, mesh, "head", 1)
    (from_both,) = after((from_both,), both_core)
    both_plane = xor_permute(from_both, mesh, "fsdp", 1)
    token_sets = [tokens]
    token_sets += [from_ctx, ctx_plane, ctx_core, xor_permute(ctx_plane, mesh, "head", 1)]
    for array in (from_groups, groups_plane):
        token_sets.append(array)
    token_sets += [xor_permute(array, mesh, "head", 1) for array in (from_groups, groups_plane)]
    token_sets += [from_both, both_plane, both_core, xor_permute(both_plane, mesh, "head", 1)]
    decays = [tail, *(array[rows:] for array in (from_ctx, from_groups, from_both))]

    def query_block(owner, head, count):
        return lax.dynamic_slice(query_weight, (0, (owner * heads + head) * size), (depth, count * size))

    query_own = [query_block(mine, head, 1) for head in range(heads)]
    query_sent = [query_block(mine ^ 1, head, 1) for head in range(heads)]
    near_block, own, other = after(
        (query_block(mine ^ 1, 0, heads), query_own[0], query_sent[0]), both_plane
    )
    query_near = xor_permute(near_block, mesh, "ctx", 1)
    parts = [
        [xor_permute(other if flip % 2 else own, mesh, "ctx", flip) for flip in range(2, flips)]
    ]

    large, small = (pltpu.CompilerParams(vmem_limit_bytes=size << 20) for size in (38, 12))
    pieces = rows // PIECE
    column_shape = (sides, rows, heads * size)
    shapes = [
        ((sides, flips, rows, depth), jnp.bfloat16),
        (column_shape, jnp.bfloat16),
        (column_shape, jnp.bfloat16),
        ((heads, sides, pieces, size, size), jnp.float32),
        ((sides, heads, rows), jnp.float32),
        ((heads, sides, rows, size), jnp.float32),
        ((heads, sides, rows, size), jnp.float32),
        ((heads, 2, size, size), jnp.bfloat16),
    ]
    held, *memory, pair_state = pl.pallas_call(
        functools.partial(key_value_kernel, heads, size, flips),
        in_specs=[SCALARS] + [ANY] * len(token_sets) + [VMEM] * sides + [ANY],
        out_specs=[VMEM] * len(shapes),
        scratch_shapes=[
            pltpu.VMEM(packed_shape, jnp.bfloat16),
            pltpu.VMEM(log_decay.shape, jnp.float32),
            pltpu.SemaphoreType.DMA((sides, flips)),
            pltpu.SemaphoreType.DMA((flips,)),
        ],
        out_shape=[jax.ShapeDtypeStruct(*shape) for shape in shapes],
        compiler_params=large,
        cost_estimate=pl.CostEstimate(
            flops=2 * sides * rows * width * 2 * heads * size,
            bytes_accessed=2 * (sides * rows * width + width * 2 * heads * size),
            transcendentals=sides * rows * 2 * heads * size,
        ),
        name="key_value",
    )(places, *token_sets, *decays, key_value)

    before = lax.ppermute(pair_state, "ctx", [(at, at + 2) for at in range(flips - 2)])
    for head in range(1, heads):
        own, other, _ = lax.optimization_barrier((query_own[head], query_sent[head], pair_state))
        parts.append(
            [xor_permute(other if flip % 2 else own, mesh, "ctx", flip) for flip in range(2, flips)]
        )

    returned = [[] for _ in SIDES]
    for head in range(heads):
        attended = pl.pallas_call(
            functools.partial(query_kernel, head, slice(head * size, (head + 1) * size), flips),
            in_specs=[SCALARS] + [VMEM] * (1 + flips + len(memory) + 1),
            out_specs=[VMEM] * sides,
            out_shape=[jax.ShapeDtypeStruct((rows, size), jnp.bfloat16)] * sides,
            compiler_params=small,
            cost_estimate=pl.CostEstimate(
                flops=2 * sides * rows * size * (width + 4 * size),
                bytes_accessed=2 * (sides * rows * width + width * size),
                transcendentals=sides * rows * 4 * size,
            ),
            name="query",
        )(places, held, query_own[head], query_near, *parts[head], *memory, before)
        returned[0].append(attended[0])
        returned[1].append(xor_permute(attended[1], mesh, "ctx", 1))
        returned[2].append(xor_permute(attended[2], mesh, "groups", 1))
        returned[3].append(lax.ppermute(attended[3], ("groups", "ctx"), both))

    flat = [piece for side in returned for piece in side]
    return pl.pallas_call(
        functools.partial(merge_kernel, heads, size),
        in_specs=[SCALARS] + [VMEM] * len(flat),
        out_specs=VMEM,
        out_shape=jax.ShapeDtypeStruct((rows, heads_here * size), jnp.bfloat16),
        name="merge",
    )(places, *flat)


def spreads(mesh, tokens, query_weight, key_weight, value_weight, log_decay):
    sizes = tuple(mesh.shape[axis] for axis in ("groups", "ctx", "fsdp", "head"))
    if sizes != (2, 4, 2, 2):
        return False
    heads_here = log_decay.shape[0]
    depth = query_weight.shape[0]
    size = query_weight.shape[1] // heads_here
    return (
        heads_here % 4 == 0
        and size == PIECE
        and depth % 128 == 0
        and depth * 4 == tokens.shape[1]
        and tokens.shape[0] % PIECE == 0
        and tokens.shape[0] <= 512
    )


def local_body(mesh, *arrays):
    if spreads(mesh, *arrays):
        return spread_body(mesh, *arrays)
    return body(*arrays)


def solution(mesh):
    return jax.shard_map(
        functools.partial(local_body, mesh),
        mesh=mesh,
        in_specs=(
            P(("groups", "ctx"), None),
            P("ctx", ("fsdp", "head")),
            P("ctx", ("fsdp", "head")),
            P("ctx", ("fsdp", "head")),
            P(("fsdp", "head"), ("groups", "ctx")),
        ),
        out_specs=P(("groups", "ctx"), ("fsdp", "head")),
        check_vma=False,
    )
```

```python
import functools
import jax
import jax.numpy as jnp
from jax import lax
from jax.experimental import pallas as pl
from jax.experimental.pallas import tpu as pltpu
from jax.sharding import PartitionSpec as P

EPSILON = 1e-06


def prefix(shard, axis, join, neutral):
    place = lax.axis_index(axis)
    gathered = jax.tree.map(
        lambda a, kind: lax.all_gather(a.astype(kind), axis), shard, (jnp.bfloat16, jnp.bfloat16)
    )
    state = jax.tree.map(lambda a, e: jnp.zeros_like(a) + jnp.asarray(e, a.dtype), shard, neutral)

    def one(turn, state):
        return join(
            state,
            jax.tree.map(
                lambda a, own: lax.dynamic_index_in_dim(a, turn, 0, False).astype(own.dtype),
                gathered,
                shard,
            ),
        )

    return lax.fori_loop(0, place, one, state)


def row_folder(tokens):

    def accumulate(running, portions, offset):
        return tuple(
            (jnp.dot(tokens, portion, preferred_element_type=jnp.float32) for portion in portions)
        )

    return accumulate


def combine_states(earlier, later):
    return (earlier[0] + later[0], jnp.exp(later[0])[:, None, None] * earlier[1] + later[1])


def local_summary(key_rows, value_rows, cumulative):
    heads_here, row_count = cumulative.shape
    head_size = key_rows.shape[1] // heads_here
    to_end = jnp.exp(cumulative[:, -1:] - cumulative)
    scaled = (
        key_rows.reshape(row_count, heads_here, head_size).astype(jnp.float32)
        * to_end.T[:, :, None]
    ).astype(jnp.bfloat16)
    valueset = value_rows.reshape(row_count, heads_here, head_size)
    return jnp.einsum("khd,khe->hde", scaled, valueset, preferred_element_type=jnp.float32)


def carried(total_decay, own_state):
    identity = (jnp.zeros_like(total_decay), jnp.zeros_like(own_state))
    return prefix((total_decay, own_state), "ctx", combine_states, identity)


def attend(query_rows, key_rows, value_rows, cumulative, incoming):
    heads_here, row_count = cumulative.shape
    head_size = query_rows.shape[1] // heads_here
    block_rows = min(row_count, 512)
    queries = query_rows.reshape(row_count, heads_here, head_size)
    keyset = key_rows.reshape(row_count, heads_here, head_size)
    valueset = value_rows.reshape(row_count, heads_here, head_size)
    incoming_bf = incoming.astype(jnp.bfloat16)
    key_index = jnp.arange(row_count)

    def one_block(block_index):
        first_row = block_index * block_rows
        query_index = first_row + jnp.arange(block_rows)
        scores = jnp.einsum("qhd,khd->hqk", queries, keyset, preferred_element_type=jnp.float32)
        causal = key_index[None, :] <= query_index[:, None]
        decay_gaps = jnp.where(
            causal[None], cumulative[:, :, None] - cumulative[:, None, :], -jnp.inf
        )
        weights = (scores * jnp.exp(decay_gaps)).astype(jnp.bfloat16)
        within_part = jnp.einsum(
            "hqk,khe->qhe", weights, valueset, preferred_element_type=jnp.float32
        )
        carried_part = (
            jnp.einsum("qhd,hde->qhe", queries, incoming_bf, preferred_element_type=jnp.float32)
            * jnp.exp(cumulative).T[:, :, None]
        )
        raw_out = within_part + carried_part
        inverse_rms = lax.rsqrt(jnp.mean(raw_out * raw_out, axis=-1, keepdims=True) + EPSILON)
        return (raw_out * inverse_rms).astype(jnp.bfloat16)

    blocks = lax.map(one_block, jnp.arange(row_count // block_rows))
    return blocks.reshape(row_count, heads_here * head_size)


def body(tokens, query_weight, key_weight, value_weight, log_decay):
    row_count = tokens.shape[0]
    zero_rows = jnp.zeros((row_count, query_weight.shape[1]), jnp.float32)
    accumulate = row_folder(tokens)
    cumulative = jnp.cumsum(log_decay, axis=1)
    total_decay = cumulative[:, -1]
    query_sum, key_sum, value_sum = accumulate(
        (zero_rows, zero_rows, zero_rows),
        (
            lax.all_gather(query_weight, "ctx", axis=0, tiled=True),
            lax.all_gather(key_weight, "ctx", axis=0, tiled=True),
            lax.all_gather(value_weight, "ctx", axis=0, tiled=True),
        ),
        jnp.int32(0),
    )
    query_rows = jax.nn.silu(query_sum).astype(jnp.bfloat16)
    key_rows = jax.nn.silu(key_sum).astype(jnp.bfloat16)
    value_rows = value_sum.astype(jnp.bfloat16)
    incoming = carried(total_decay, local_summary(key_rows, value_rows, cumulative))[1]
    return attend(query_rows, key_rows, value_rows, cumulative, incoming)


SIDES = ("own", "ctx", "groups", "both")
PIECE = 128
ANY = pl.BlockSpec(memory_space=pl.ANY)
VMEM = pl.BlockSpec(memory_space=pltpu.VMEM)
SCALARS = pl.BlockSpec(memory_space=pltpu.SMEM)


def xor_permute(array, mesh, axis, flip):
    return lax.ppermute(array, axis, [(at, at ^ flip) for at in range(mesh.shape[axis])])


def after(arrays, *earlier):
    return lax.optimization_barrier((*arrays, *earlier))[: len(arrays)]


def in_three(array):
    parts = []
    for _ in range(3):
        part = lax.reduce_precision(array, 8, 7)
        parts.append(part.astype(jnp.bfloat16))
        array = array - part
    return jnp.concatenate(parts, axis=0)


def silu(rows):
    return rows / (1.0 + jnp.exp(-rows))


def running_sum(rows):
    lane = lax.broadcasted_iota(jnp.int32, rows.shape, 1)
    shift = 1
    while shift < rows.shape[1]:
        rows += jnp.where(lane >= shift, pltpu.roll(rows, shift, 1), 0.0)
        shift *= 2
    return rows


def column_of(row):
    return jnp.transpose(jnp.broadcast_to(row, (PIECE, row.shape[1])))


def token_copies(places, token_refs, held, semaphores):
    turn, share = places[0], places[1] * 2 + places[2]
    own_ref, quarter_refs = token_refs[0], token_refs[1:]
    width = held.shape[3]

    def copy(source, side, flip):
        return pltpu.make_async_copy(source, held.at[side, flip], semaphores.at[side, flip])

    def start():
        for side in range(len(SIDES)):
            for flip in range(held.shape[1]):
                block = turn ^ flip
                if side == 0:
                    at = pl.multiple_of(block * width, width)
                    copy(own_ref.at[:, pl.ds(at, width)], side, flip).start()
                    continue
                for place, ref in enumerate(quarter_refs[4 * (side - 1) : 4 * side]):

                    @pl.when(block ^ share == place)
                    def _(ref=ref):
                        copy(ref.at[0 : held.shape[2], :], side, flip).start()

    def wait(side):
        for flip in range(held.shape[1]):
            copy(quarter_refs[0].at[0 : held.shape[2], :], side, flip).wait()

    return start, wait


def project(token_refs, weights):
    total = None
    for token_ref, weight in zip(token_refs, weights):
        product = jnp.dot(token_ref[...], weight, preferred_element_type=jnp.float32)
        total = product if total is None else total + product
    return total


def piece_rows(rows):
    return [slice(at, at + PIECE) for at in range(0, rows, PIECE)]


def key_value_kernel(heads, size, flips, places, *refs):
    sides = len(SIDES)
    token_refs, refs = refs[:13], refs[13:]
    decay_refs, refs = refs[:sides], refs[sides:]
    source_ref, held, key_ref, value_ref, state_ref, sum_ref, fade_ref, mask_ref, pair_ref = refs[:9]
    weight_ref, decay_ref, semaphores, weight_semaphores = refs[9:]
    loads = [
        pltpu.make_async_copy(
            source_ref.at[places[0] ^ flip], weight_ref.at[flip], weight_semaphores.at[flip]
        )
        for flip in range(flips)
    ]
    for load in loads:
        load.start()
    start, wait = token_copies(places, token_refs, held, semaphores)
    start()
    odd = places[0] % 2 == 1
    causal = lax.broadcasted_iota(jnp.int32, (PIECE, PIECE), 1) <= lax.broadcasted_iota(
        jnp.int32, (PIECE, PIECE), 0
    )
    cuts = piece_rows(key_ref.shape[1])
    for side in range(sides):
        part = decay_refs[side][...].astype(jnp.float32)
        count = part.shape[0] // 3
        log_decay = part[:count] + (part[count : 2 * count] + part[2 * count :])
        decay_ref[...] = running_sum(log_decay[:, : sum_ref.shape[2]])
        for head in range(heads):
            sum_ref[side, head : head + 1, :] = decay_ref[pl.ds(places[3] * heads + head, 1), :]
    for load in loads:
        load.wait()
    for side in range(sides):
        wait(side)
        for head in range(heads):
            at = slice(2 * head * size, 2 * (head + 1) * size)
            both = project(
                [held.at[side, flip] for flip in range(flips)],
                [weight_ref[flip, :, at] for flip in range(flips)],
            )
            key = silu(both[:, :size])
            key_bf = key.astype(jnp.bfloat16)
            key = key_bf.astype(jnp.float32)
            value = both[:, size:].astype(jnp.bfloat16)
            key_ref[side, :, head * size : (head + 1) * size] = key_bf
            value_ref[side, :, head * size : (head + 1) * size] = value
            row = sum_ref[side, head : head + 1, :]
            column = column_of(row)
            ends = [column[cut.stop - 1 : cut.stop, :] for cut in cuts]
            fresh = []
            for cut, end in zip(cuts, ends):
                scaled = (key[cut] * jnp.exp(end - column[cut])).astype(jnp.bfloat16)
                fresh.append(
                    lax.dot_general(
                        scaled, value[cut], (((0,), (0,)), ((), ())), preferred_element_type=jnp.float32
                    )
                )
            state = fresh[0]
            for piece, cut in enumerate(cuts):
                begin = ends[piece - 1] if piece else jnp.zeros_like(ends[0])
                if piece:
                    state = jnp.exp(ends[piece] - begin) * state + fresh[piece]
                state_ref[head, side, piece] = state
                fade_ref[head, side, cut, :] = jnp.exp(column[cut] - begin)
                gaps = jnp.where(causal, column[cut] - row[:, cut], -jnp.inf)
                mask_ref[head, side, cut, :] = jnp.exp(gaps)
    last = len(cuts) - 1
    end = sum_ref.shape[2] - 1
    for head in range(heads):
        for pair in range(2):
            own, other = state_ref[head, 2 * pair, last], state_ref[head, 2 * pair + 1, last]
            own_total = sum_ref[2 * pair, head : head + 1, end:]
            other_total = sum_ref[2 * pair + 1, head : head + 1, end:]
            total = jnp.where(odd, own_total, other_total)
            first, second = jnp.where(odd, other, own), jnp.where(odd, own, other)
            pair_ref[head, pair] = (jnp.exp(total) * first + second).astype(jnp.bfloat16)


def query_kernel(head, columns, flips, places, *refs):
    sides = len(SIDES)
    held, refs = refs[0], refs[1:]
    weight_refs, refs = refs[:flips], refs[flips:]
    key_ref, value_ref, state_ref, sum_ref, fade_ref, mask_ref, before_ref = refs[:7]
    out_refs = refs[7:]
    odd = places[0] % 2 == 1
    cuts = piece_rows(key_ref.shape[1])
    last = len(cuts) - 1
    end = sum_ref.shape[2] - 1
    for side in range(sides):
        partner = side ^ 1
        before = before_ref[head, side // 2].astype(jnp.float32)
        total = sum_ref[partner, head : head + 1, end:]
        later = jnp.exp(total) * before + state_ref[head, partner, last]
        second = odd if side % 2 == 0 else jnp.logical_not(odd)
        incoming = jnp.where(second, later, before)
        states = [incoming.astype(jnp.bfloat16)]
        for piece in range(1, len(cuts)):
            stop = cuts[piece].start - 1
            sofar = jnp.exp(sum_ref[side, head : head + 1, stop : stop + 1])
            states.append((state_ref[head, side, piece - 1] + sofar * incoming).astype(jnp.bfloat16))
        query = project(
            [held.at[side, flip] for flip in range(flips)],
            [ref[:, columns] if flip == 1 else ref[...] for flip, ref in enumerate(weight_refs)],
        )
        query = silu(query).astype(jnp.bfloat16)
        at = slice(head * PIECE, (head + 1) * PIECE)
        weights = [
            (
                lax.dot_general(
                    query[cut],
                    key_ref[side, cut, at],
                    (((1,), (1,)), ((), ())),
                    preferred_element_type=jnp.float32,
                )
                * mask_ref[head, side, cut, :]
            ).astype(jnp.bfloat16)
            for cut in cuts
        ]
        raws = [
            jnp.dot(query[cut], state, preferred_element_type=jnp.float32) * fade_ref[head, side, cut, :]
            for cut, state in zip(cuts, states)
        ]
        raws = [
            raw + jnp.dot(weight, value_ref[side, cut, at], preferred_element_type=jnp.float32)
            for raw, weight, cut in zip(raws, weights, cuts)
        ]
        for raw, cut in zip(raws, cuts):
            scale = lax.rsqrt(jnp.mean(raw * raw, axis=1, keepdims=True) + EPSILON)
            out_refs[side][cut, :] = (raw * scale).astype(jnp.bfloat16)


def merge_kernel(heads, size, places, *refs):
    pieces, out_ref = refs[:-1], refs[-1]
    for side in range(len(SIDES)):
        for head in range(heads):
            at = pl.multiple_of(((places[3] ^ side) * heads + head) * size, size)
            out_ref[:, pl.ds(at, size)] = pieces[side * heads + head][...]


def pack_kernel(heads, size, places, key_ref, value_ref, out_ref):
    for head in range(heads):
        at, to = head * size, 2 * head * size
        out_ref[0, :, to : to + size] = key_ref[:, at : at + size]
        out_ref[0, :, to + size : to + 2 * size] = value_ref[:, at : at + size]


def spread_body(mesh, tokens, query_weight, key_weight, value_weight, log_decay):
    rows, width = tokens.shape
    depth = query_weight.shape[0]
    heads_here = log_decay.shape[0]
    size = query_weight.shape[1] // heads_here
    flips = mesh.shape["ctx"]
    heads = heads_here // 4
    sides = len(SIDES)
    group, turn = lax.axis_index("groups"), lax.axis_index("ctx")
    plane, core = lax.axis_index("fsdp"), lax.axis_index("head")
    mine = group * 2 + turn % 2
    places = jnp.stack([turn, core, plane, mine]).astype(jnp.int32)
    both = [
        (at, (at // flips ^ 1) * flips + (at % flips ^ 1)) for at in range(mesh.shape["groups"] * flips)
    ]

    share = core * 2 + plane
    quarter = lax.dynamic_slice(tokens, (0, share * depth), (rows, depth))
    tail = jnp.pad(in_three(log_decay), ((0, 0), (0, depth - rows)))
    quarter = jnp.concatenate([quarter, tail], axis=0)
    beside = lax.dynamic_slice(tokens, (0, (share ^ 1) * depth), (rows, depth))

    block = (depth, heads * size)
    packed_shape = (flips, depth, 2 * heads * size)
    owner = pl.BlockSpec(block, lambda step, places: (0, places[3] ^ ((places[0] ^ step) % 2)))
    packed = pl.pallas_call(
        functools.partial(pack_kernel, heads, size),
        grid_spec=pltpu.PrefetchScalarGridSpec(
            num_scalar_prefetch=1,
            grid=(flips,),
            in_specs=[owner, owner],
            out_specs=pl.BlockSpec((1,) + packed_shape[1:], lambda step, places: (step, 0, 0)),
        ),
        out_shape=jax.ShapeDtypeStruct(packed_shape, jnp.bfloat16),
        cost_estimate=pl.CostEstimate(flops=0, bytes_accessed=32 * depth * heads * size, transcendentals=0),
        name="pack",
    )(places, key_weight, value_weight)

    key_value = lax.all_to_all(packed, "ctx", 0, 0)

    from_ctx = xor_permute(quarter, mesh, "ctx", 1)
    from_groups = xor_permute(quarter, mesh, "groups", 1)
    ctx_core = xor_permute(from_ctx, mesh, "head", 1)
    (from_ctx,) = after((from_ctx,), ctx_core, from_groups)
    ctx_plane = xor_permute(from_ctx, mesh, "fsdp", 1)
    from_both = xor_permute(from_ctx, mesh, "groups", 1)
    groups_plane = xor_permute(after((beside,), from_ctx)[0], mesh, "groups", 1)
    both_core = xor_permute(from_both, mesh, "head", 1)
    (from_both,) = after((from_both,), both_core, ctx_plane)
    both_plane = xor_permute(from_both, mesh, "fsdp", 1)
    (both_plane,) = after((both_plane,), groups_plane)
    token_sets = [tokens]
    token_sets += [from_ctx, ctx_plane, ctx_core, xor_permute(ctx_plane, mesh, "head", 1)]
    for array in (from_groups, groups_plane):
        token_sets.append(array)
    token_sets += [xor_permute(array, mesh, "head", 1) for array in (from_groups, groups_plane)]
    token_sets += [from_both, both_plane, both_core, xor_permute(both_plane, mesh, "head", 1)]
    decays = [tail, *(array[rows:] for array in (from_ctx, from_groups, from_both))]

    def query_block(owner, head, count):
        return lax.dynamic_slice(query_weight, (0, (owner * heads + head) * size), (depth, count * size))

    query_own = [query_block(mine, head, 1) for head in range(heads)]
    query_sent = [query_block(mine ^ 1, head, 1) for head in range(heads)]
    near_block, own, other = after(
        (query_block(mine ^ 1, 0, heads), query_own[0], query_sent[0]), both_plane
    )
    query_near = xor_permute(near_block, mesh, "ctx", 1)
    parts = [
        [xor_permute(other if flip % 2 else own, mesh, "ctx", flip) for flip in range(2, flips)]
    ]

    large, small = (pltpu.CompilerParams(vmem_limit_bytes=size << 20) for size in (38, 12))
    pieces = rows // PIECE
    column_shape = (sides, rows, heads * size)
    shapes = [
        ((sides, flips, rows, depth), jnp.bfloat16),
        (column_shape, jnp.bfloat16),
        (column_shape, jnp.bfloat16),
        ((heads, sides, pieces, size, size), jnp.float32),
        ((sides, heads, rows), jnp.float32),
        ((heads, sides, rows, size), jnp.float32),
        ((heads, sides, rows, size), jnp.float32),
        ((heads, 2, size, size), jnp.bfloat16),
    ]
    held, *memory, pair_state = pl.pallas_call(
        functools.partial(key_value_kernel, heads, size, flips),
        in_specs=[SCALARS] + [ANY] * len(token_sets) + [VMEM] * sides + [ANY],
        out_specs=[VMEM] * len(shapes),
        scratch_shapes=[
            pltpu.VMEM(packed_shape, jnp.bfloat16),
            pltpu.VMEM(log_decay.shape, jnp.float32),
            pltpu.SemaphoreType.DMA((sides, flips)),
            pltpu.SemaphoreType.DMA((flips,)),
        ],
        out_shape=[jax.ShapeDtypeStruct(*shape) for shape in shapes],
        compiler_params=large,
        cost_estimate=pl.CostEstimate(
            flops=2 * sides * rows * width * 2 * heads * size,
            bytes_accessed=2 * (sides * rows * width + width * 2 * heads * size),
            transcendentals=sides * rows * 2 * heads * size,
        ),
        name="key_value",
    )(places, *token_sets, *decays, key_value)

    before = lax.ppermute(pair_state, "ctx", [(at, at + 2) for at in range(flips - 2)])
    for head in range(1, heads):
        own, other, _ = lax.optimization_barrier((query_own[head], query_sent[head], pair_state))
        parts.append(
            [xor_permute(other if flip % 2 else own, mesh, "ctx", flip) for flip in range(2, flips)]
        )

    returned = [[] for _ in SIDES]
    for head in range(heads):
        attended = pl.pallas_call(
            functools.partial(query_kernel, head, slice(head * size, (head + 1) * size), flips),
            in_specs=[SCALARS] + [VMEM] * (1 + flips + len(memory) + 1),
            out_specs=[VMEM] * sides,
            out_shape=[jax.ShapeDtypeStruct((rows, size), jnp.bfloat16)] * sides,
            compiler_params=small,
            cost_estimate=pl.CostEstimate(
                flops=2 * sides * rows * size * (width + 4 * size),
                bytes_accessed=2 * (sides * rows * width + width * size),
                transcendentals=sides * rows * 4 * size,
            ),
            name="query",
        )(places, held, query_own[head], query_near, *parts[head], *memory, before)
        returned[0].append(attended[0])
        returned[1].append(xor_permute(attended[1], mesh, "ctx", 1))
        returned[2].append(xor_permute(attended[2], mesh, "groups", 1))
        returned[3].append(lax.ppermute(attended[3], ("groups", "ctx"), both))

    flat = [piece for side in returned for piece in side]
    return pl.pallas_call(
        functools.partial(merge_kernel, heads, size),
        in_specs=[SCALARS] + [VMEM] * len(flat),
        out_specs=VMEM,
        out_shape=jax.ShapeDtypeStruct((rows, heads_here * size), jnp.bfloat16),
        name="merge",
    )(places, *flat)


def spreads(mesh, tokens, query_weight, key_weight, value_weight, log_decay):
    sizes = tuple(mesh.shape[axis] for axis in ("groups", "ctx", "fsdp", "head"))
    if sizes != (2, 4, 2, 2):
        return False
    heads_here = log_decay.shape[0]
    depth = query_weight.shape[0]
    size = query_weight.shape[1] // heads_here
    return (
        heads_here % 4 == 0
        and size == PIECE
        and depth % 128 == 0
        and depth * 4 == tokens.shape[1]
        and tokens.shape[0] % PIECE == 0
        and tokens.shape[0] <= 512
    )


def local_body(mesh, *arrays):
    if spreads(mesh, *arrays):
        return spread_body(mesh, *arrays)
    return body(*arrays)


def solution(mesh):
    return jax.shard_map(
        functools.partial(local_body, mesh),
        mesh=mesh,
        in_specs=(
            P(("groups", "ctx"), None),
            P("ctx", ("fsdp", "head")),
            P("ctx", ("fsdp", "head")),
            P("ctx", ("fsdp", "head")),
            P(("fsdp", "head"), ("groups", "ctx")),
        ),
        out_specs=P(("groups", "ctx"), ("fsdp", "head")),
        check_vma=False,
    )
```

```python
import functools
import jax
import jax.numpy as jnp
from jax import lax
from jax.experimental import pallas as pl
from jax.experimental.pallas import tpu as pltpu
from jax.sharding import PartitionSpec as P

EPSILON = 1e-06


def prefix(shard, axis, join, neutral):
    place = lax.axis_index(axis)
    gathered = jax.tree.map(
        lambda a, kind: lax.all_gather(a.astype(kind), axis), shard, (jnp.bfloat16, jnp.bfloat16)
    )
    state = jax.tree.map(lambda a, e: jnp.zeros_like(a) + jnp.asarray(e, a.dtype), shard, neutral)

    def one(turn, state):
        return join(
            state,
            jax.tree.map(
                lambda a, own: lax.dynamic_index_in_dim(a, turn, 0, False).astype(own.dtype),
                gathered,
                shard,
            ),
        )

    return lax.fori_loop(0, place, one, state)


def row_folder(tokens):

    def accumulate(running, portions, offset):
        return tuple(
            (jnp.dot(tokens, portion, preferred_element_type=jnp.float32) for portion in portions)
        )

    return accumulate


def combine_states(earlier, later):
    return (earlier[0] + later[0], jnp.exp(later[0])[:, None, None] * earlier[1] + later[1])


def local_summary(key_rows, value_rows, cumulative):
    heads_here, row_count = cumulative.shape
    head_size = key_rows.shape[1] // heads_here
    to_end = jnp.exp(cumulative[:, -1:] - cumulative)
    scaled = (
        key_rows.reshape(row_count, heads_here, head_size).astype(jnp.float32)
        * to_end.T[:, :, None]
    ).astype(jnp.bfloat16)
    valueset = value_rows.reshape(row_count, heads_here, head_size)
    return jnp.einsum("khd,khe->hde", scaled, valueset, preferred_element_type=jnp.float32)


def carried(total_decay, own_state):
    identity = (jnp.zeros_like(total_decay), jnp.zeros_like(own_state))
    return prefix((total_decay, own_state), "ctx", combine_states, identity)


def attend(query_rows, key_rows, value_rows, cumulative, incoming):
    heads_here, row_count = cumulative.shape
    head_size = query_rows.shape[1] // heads_here
    block_rows = min(row_count, 512)
    queries = query_rows.reshape(row_count, heads_here, head_size)
    keyset = key_rows.reshape(row_count, heads_here, head_size)
    valueset = value_rows.reshape(row_count, heads_here, head_size)
    incoming_bf = incoming.astype(jnp.bfloat16)
    key_index = jnp.arange(row_count)

    def one_block(block_index):
        first_row = block_index * block_rows
        query_index = first_row + jnp.arange(block_rows)
        scores = jnp.einsum("qhd,khd->hqk", queries, keyset, preferred_element_type=jnp.float32)
        causal = key_index[None, :] <= query_index[:, None]
        decay_gaps = jnp.where(
            causal[None], cumulative[:, :, None] - cumulative[:, None, :], -jnp.inf
        )
        weights = (scores * jnp.exp(decay_gaps)).astype(jnp.bfloat16)
        within_part = jnp.einsum(
            "hqk,khe->qhe", weights, valueset, preferred_element_type=jnp.float32
        )
        carried_part = (
            jnp.einsum("qhd,hde->qhe", queries, incoming_bf, preferred_element_type=jnp.float32)
            * jnp.exp(cumulative).T[:, :, None]
        )
        raw_out = within_part + carried_part
        inverse_rms = lax.rsqrt(jnp.mean(raw_out * raw_out, axis=-1, keepdims=True) + EPSILON)
        return (raw_out * inverse_rms).astype(jnp.bfloat16)

    blocks = lax.map(one_block, jnp.arange(row_count // block_rows))
    return blocks.reshape(row_count, heads_here * head_size)


def body(tokens, query_weight, key_weight, value_weight, log_decay):
    row_count = tokens.shape[0]
    zero_rows = jnp.zeros((row_count, query_weight.shape[1]), jnp.float32)
    accumulate = row_folder(tokens)
    cumulative = jnp.cumsum(log_decay, axis=1)
    total_decay = cumulative[:, -1]
    query_sum, key_sum, value_sum = accumulate(
        (zero_rows, zero_rows, zero_rows),
        (
            lax.all_gather(query_weight, "ctx", axis=0, tiled=True),
            lax.all_gather(key_weight, "ctx", axis=0, tiled=True),
            lax.all_gather(value_weight, "ctx", axis=0, tiled=True),
        ),
        jnp.int32(0),
    )
    query_rows = jax.nn.silu(query_sum).astype(jnp.bfloat16)
    key_rows = jax.nn.silu(key_sum).astype(jnp.bfloat16)
    value_rows = value_sum.astype(jnp.bfloat16)
    incoming = carried(total_decay, local_summary(key_rows, value_rows, cumulative))[1]
    return attend(query_rows, key_rows, value_rows, cumulative, incoming)


SIDES = ("own", "ctx", "groups", "both")
PIECE = 128
ANY = pl.BlockSpec(memory_space=pl.ANY)
VMEM = pl.BlockSpec(memory_space=pltpu.VMEM)
SCALARS = pl.BlockSpec(memory_space=pltpu.SMEM)


def xor_permute(array, mesh, axis, flip):
    return lax.ppermute(array, axis, [(at, at ^ flip) for at in range(mesh.shape[axis])])


def after(arrays, *earlier):
    return lax.optimization_barrier((*arrays, *earlier))[: len(arrays)]


def in_three(array):
    parts = []
    for _ in range(3):
        part = lax.reduce_precision(array, 8, 7)
        parts.append(part.astype(jnp.bfloat16))
        array = array - part
    return jnp.concatenate(parts, axis=0)


def silu(rows):
    return rows / (1.0 + jnp.exp(-rows))


def running_sum(rows):
    lane = lax.broadcasted_iota(jnp.int32, rows.shape, 1)
    shift = 1
    while shift < rows.shape[1]:
        rows += jnp.where(lane >= shift, pltpu.roll(rows, shift, 1), 0.0)
        shift *= 2
    return rows


def column_of(row):
    return jnp.transpose(jnp.broadcast_to(row, (PIECE, row.shape[1])))


def token_copies(places, token_refs, held, semaphores):
    turn, share = places[0], places[1] * 2 + places[2]
    own_ref, quarter_refs = token_refs[0], token_refs[1:]
    width = held.shape[3]

    def copy(source, side, flip):
        return pltpu.make_async_copy(source, held.at[side, flip], semaphores.at[side, flip])

    def start():
        for side in range(len(SIDES)):
            for flip in range(held.shape[1]):
                block = turn ^ flip
                if side == 0:
                    at = pl.multiple_of(block * width, width)
                    copy(own_ref.at[:, pl.ds(at, width)], side, flip).start()
                    continue
                for place, ref in enumerate(quarter_refs[4 * (side - 1) : 4 * side]):

                    @pl.when(block ^ share == place)
                    def _(ref=ref):
                        copy(ref.at[0 : held.shape[2], :], side, flip).start()

    def wait(side):
        for flip in range(held.shape[1]):
            copy(quarter_refs[0].at[0 : held.shape[2], :], side, flip).wait()

    return start, wait


def project(held, side, cut, weights):
    total = None
    for flip, weight in enumerate(weights):
        product = jnp.dot(held[side, flip, cut, :], weight, preferred_element_type=jnp.float32)
        total = product if total is None else total + product
    return total


def piece_rows(rows):
    return [slice(at, at + PIECE) for at in range(0, rows, PIECE)]


def staggered(items, *stages):
    carried = {}
    for turn in range(len(items) + len(stages) - 1):
        for depth in reversed(range(len(stages))):
            at = turn - depth
            if 0 <= at < len(items):
                carried[at] = stages[depth](items[at], carried.get(at))


def key_value_kernel(heads, size, flips, places, *refs):
    sides = len(SIDES)
    token_refs, refs = refs[:13], refs[13:]
    decay_refs, refs = refs[:sides], refs[sides:]
    source_ref, held, key_ref, value_ref, state_ref, sum_ref, fade_ref, mask_ref, pair_ref = refs[:9]
    weight_ref, decay_ref, end_ref, semaphores, weight_semaphores = refs[9:]
    loads = [
        pltpu.make_async_copy(
            source_ref.at[places[0] ^ flip], weight_ref.at[flip], weight_semaphores.at[flip]
        )
        for flip in range(flips)
    ]
    for load in loads:
        load.start()
    start, wait = token_copies(places, token_refs, held, semaphores)
    start()
    odd = places[0] % 2 == 1
    causal = lax.broadcasted_iota(jnp.int32, (PIECE, PIECE), 1) <= lax.broadcasted_iota(
        jnp.int32, (PIECE, PIECE), 0
    )
    cuts = piece_rows(key_ref.shape[1])
    for side in range(sides):
        part = decay_refs[side][...].astype(jnp.float32)
        count = part.shape[0] // 3
        log_decay = part[:count] + (part[count : 2 * count] + part[2 * count :])
        decay_ref[...] = running_sum(log_decay[:, : sum_ref.shape[2]])
        for head in range(heads):
            row = decay_ref[pl.ds(places[3] * heads + head, 1), :]
            sum_ref[side, head : head + 1, :] = row
            column = column_of(row)
            begin = jnp.zeros_like(column[:1])
            for cut in cuts:
                end = column[cut.stop - 1 : cut.stop, :]
                end_ref[head, side, cut, :] = jnp.exp(end - column[cut])
                fade_ref[head, side, cut, :] = jnp.exp(column[cut] - begin)
                gaps = jnp.where(causal, column[cut] - row[:, cut], -jnp.inf)
                mask_ref[head, side, cut, :] = jnp.exp(gaps)
                begin = end
    for load in loads:
        load.wait()

    def first(item, _):
        side, head, piece = item
        if head == 0 and piece == 0:
            wait(side)
        at = slice(2 * head * size, 2 * (head + 1) * size)
        return project(held, side, cuts[piece], [weight_ref[flip, :, at] for flip in range(flips)])

    def second(item, both):
        side, head, piece = item
        cut, to = cuts[piece], slice(head * size, (head + 1) * size)
        key = silu(both[:, :size]).astype(jnp.bfloat16)
        value = both[:, size:].astype(jnp.bfloat16)
        key_ref[side, cut, to] = key
        value_ref[side, cut, to] = value
        scaled = (key.astype(jnp.float32) * end_ref[head, side, cut, :]).astype(jnp.bfloat16)
        return scaled, value

    def third(item, pair):
        side, head, piece = item
        state = lax.dot_general(
            pair[0], pair[1], (((0,), (0,)), ((), ())), preferred_element_type=jnp.float32
        )
        if piece:
            sums, cut = sum_ref[side, head : head + 1, :], cuts[piece]
            fade = sums[:, cut.stop - 1 : cut.stop] - sums[:, cut.start - 1 : cut.start]
            state += jnp.exp(fade) * state_ref[head, side, piece - 1]
        state_ref[head, side, piece] = state

    staggered(
        [(side, head, piece) for side in range(sides) for head in range(heads) for piece in range(len(cuts))],
        first,
        second,
        third,
    )
    last = len(cuts) - 1
    end = sum_ref.shape[2] - 1
    for head in range(heads):
        for pair in range(2):
            own, other = state_ref[head, 2 * pair, last], state_ref[head, 2 * pair + 1, last]
            own_total = sum_ref[2 * pair, head : head + 1, end:]
            other_total = sum_ref[2 * pair + 1, head : head + 1, end:]
            total = jnp.where(odd, own_total, other_total)
            first, second = jnp.where(odd, other, own), jnp.where(odd, own, other)
            pair_ref[head, pair] = (jnp.exp(total) * first + second).astype(jnp.bfloat16)


def query_kernel(head, columns, flips, places, *refs):
    sides = len(SIDES)
    held, refs = refs[0], refs[1:]
    weight_refs, refs = refs[:flips], refs[flips:]
    key_ref, value_ref, state_ref, sum_ref, fade_ref, mask_ref, before_ref = refs[:7]
    out_refs, incoming_ref = refs[7:-1], refs[-1]
    odd = places[0] % 2 == 1
    cuts = piece_rows(key_ref.shape[1])
    last = len(cuts) - 1
    end = sum_ref.shape[2] - 1
    at = slice(head * PIECE, (head + 1) * PIECE)
    weights = [ref[:, columns] if flip == 1 else ref[...] for flip, ref in enumerate(weight_refs)]
    for side in range(sides):
        partner = side ^ 1
        before = before_ref[head, side // 2].astype(jnp.float32)
        total = sum_ref[partner, head : head + 1, end:]
        later = jnp.exp(total) * before + state_ref[head, partner, last]
        second = odd if side % 2 == 0 else jnp.logical_not(odd)
        incoming = jnp.where(second, later, before)
        for piece, cut in enumerate(cuts):
            state = incoming
            if piece:
                sofar = jnp.exp(sum_ref[side, head : head + 1, cut.start - 1 : cut.start])
                state = state_ref[head, side, piece - 1] + sofar * incoming
            incoming_ref[side, piece] = state.astype(jnp.bfloat16)

    def first(item, _):
        side, piece = item
        return silu(project(held, side, cuts[piece], weights)).astype(jnp.bfloat16)

    def second(item, query):
        side, cut = item[0], cuts[item[1]]
        scores = lax.dot_general(
            query, key_ref[side, cut, at], (((1,), (1,)), ((), ())), preferred_element_type=jnp.float32
        )
        raw = jnp.dot(query, incoming_ref[side, item[1]], preferred_element_type=jnp.float32)
        return (scores * mask_ref[head, side, cut, :]).astype(jnp.bfloat16), raw * fade_ref[head, side, cut, :]

    def third(item, pair):
        side, cut = item[0], cuts[item[1]]
        return pair[1] + jnp.dot(pair[0], value_ref[side, cut, at], preferred_element_type=jnp.float32)

    def fourth(item, raw):
        side, cut = item[0], cuts[item[1]]
        scale = lax.rsqrt(jnp.mean(raw * raw, axis=1, keepdims=True) + EPSILON)
        out_refs[side][cut, :] = (raw * scale).astype(jnp.bfloat16)

    staggered(
        [(side, piece) for side in range(sides) for piece in range(len(cuts))], first, second, third, fourth
    )


def merge_kernel(heads, size, places, *refs):
    pieces, out_ref = refs[:-1], refs[-1]
    for side in range(len(SIDES)):
        for head in range(heads):
            at = pl.multiple_of(((places[3] ^ side) * heads + head) * size, size)
            out_ref[:, pl.ds(at, size)] = pieces[side * heads + head][...]


def pack_kernel(heads, size, places, key_ref, value_ref, out_ref):
    for head in range(heads):
        at, to = head * size, 2 * head * size
        out_ref[0, :, to : to + size] = key_ref[:, at : at + size]
        out_ref[0, :, to + size : to + 2 * size] = value_ref[:, at : at + size]


def spread_body(mesh, tokens, query_weight, key_weight, value_weight, log_decay):
    rows, width = tokens.shape
    depth = query_weight.shape[0]
    heads_here = log_decay.shape[0]
    size = query_weight.shape[1] // heads_here
    flips = mesh.shape["ctx"]
    heads = heads_here // 4
    sides = len(SIDES)
    group, turn = lax.axis_index("groups"), lax.axis_index("ctx")
    plane, core = lax.axis_index("fsdp"), lax.axis_index("head")
    mine = group * 2 + turn % 2
    places = jnp.stack([turn, core, plane, mine]).astype(jnp.int32)
    both = [
        (at, (at // flips ^ 1) * flips + (at % flips ^ 1)) for at in range(mesh.shape["groups"] * flips)
    ]

    share = core * 2 + plane
    quarter = lax.dynamic_slice(tokens, (0, share * depth), (rows, depth))
    tail = jnp.pad(in_three(log_decay), ((0, 0), (0, depth - rows)))
    quarter = jnp.concatenate([quarter, tail], axis=0)
    beside = lax.dynamic_slice(tokens, (0, (share ^ 1) * depth), (rows, depth))

    block = (depth, heads * size)
    packed_shape = (flips, depth, 2 * heads * size)
    owner = pl.BlockSpec(block, lambda step, places: (0, places[3] ^ ((places[0] ^ step) % 2)))
    packed = pl.pallas_call(
        functools.partial(pack_kernel, heads, size),
        grid_spec=pltpu.PrefetchScalarGridSpec(
            num_scalar_prefetch=1,
            grid=(flips,),
            in_specs=[owner, owner],
            out_specs=pl.BlockSpec((1,) + packed_shape[1:], lambda step, places: (step, 0, 0)),
        ),
        out_shape=jax.ShapeDtypeStruct(packed_shape, jnp.bfloat16),
        cost_estimate=pl.CostEstimate(flops=0, bytes_accessed=32 * depth * heads * size, transcendentals=0),
        name="pack",
    )(places, key_weight, value_weight)

    key_value = lax.all_to_all(packed, "ctx", 0, 0)

    from_ctx = xor_permute(quarter, mesh, "ctx", 1)
    from_groups = xor_permute(quarter, mesh, "groups", 1)
    (from_ctx,) = after((from_ctx,), from_groups)
    ctx_core = xor_permute(from_ctx, mesh, "head", 1)
    (from_ctx,) = after((from_ctx,), ctx_core)
    ctx_plane = xor_permute(from_ctx, mesh, "fsdp", 1)
    from_both = xor_permute(from_ctx, mesh, "groups", 1)
    groups_plane = xor_permute(after((beside,), from_ctx)[0], mesh, "groups", 1)
    both_core = xor_permute(from_both, mesh, "head", 1)
    (from_both,) = after((from_both,), both_core, ctx_plane)
    both_plane = xor_permute(from_both, mesh, "fsdp", 1)
    (both_plane,) = after((both_plane,), groups_plane)
    token_sets = [tokens]
    token_sets += [from_ctx, ctx_plane, ctx_core, xor_permute(ctx_plane, mesh, "head", 1)]
    for array in (from_groups, groups_plane):
        token_sets.append(array)
    token_sets += [xor_permute(array, mesh, "head", 1) for array in (from_groups, groups_plane)]
    token_sets += [from_both, both_plane, both_core, xor_permute(both_plane, mesh, "head", 1)]
    decays = [tail, *(array[rows:] for array in (from_ctx, from_groups, from_both))]

    def query_block(owner, head, count):
        return lax.dynamic_slice(query_weight, (0, (owner * heads + head) * size), (depth, count * size))

    query_own = [query_block(mine, head, 1) for head in range(heads)]
    query_sent = [query_block(mine ^ 1, head, 1) for head in range(heads)]
    near_block, own, other = after(
        (query_block(mine ^ 1, 0, heads), query_own[0], query_sent[0]), both_plane
    )
    query_near = xor_permute(near_block, mesh, "ctx", 1)
    parts = [
        [xor_permute(other if flip % 2 else own, mesh, "ctx", flip) for flip in range(2, flips)]
    ]

    large, small = (pltpu.CompilerParams(vmem_limit_bytes=size << 20) for size in (38, 12))
    pieces = rows // PIECE
    column_shape = (sides, rows, heads * size)
    shapes = [
        ((sides, flips, rows, depth), jnp.bfloat16),
        (column_shape, jnp.bfloat16),
        (column_shape, jnp.bfloat16),
        ((heads, sides, pieces, size, size), jnp.float32),
        ((sides, heads, rows), jnp.float32),
        ((heads, sides, rows, size), jnp.float32),
        ((heads, sides, rows, size), jnp.float32),
        ((heads, 2, size, size), jnp.bfloat16),
    ]
    held, *memory, pair_state = pl.pallas_call(
        functools.partial(key_value_kernel, heads, size, flips),
        in_specs=[SCALARS] + [ANY] * len(token_sets) + [VMEM] * sides + [ANY],
        out_specs=[VMEM] * len(shapes),
        scratch_shapes=[
            pltpu.VMEM(packed_shape, jnp.bfloat16),
            pltpu.VMEM(log_decay.shape, jnp.float32),
            pltpu.VMEM((heads, sides, rows, size), jnp.float32),
            pltpu.SemaphoreType.DMA((sides, flips)),
            pltpu.SemaphoreType.DMA((flips,)),
        ],
        out_shape=[jax.ShapeDtypeStruct(*shape) for shape in shapes],
        compiler_params=large,
        cost_estimate=pl.CostEstimate(
            flops=2 * sides * rows * width * 2 * heads * size,
            bytes_accessed=2 * (sides * rows * width + width * 2 * heads * size),
            transcendentals=sides * rows * 2 * heads * size,
        ),
        name="key_value",
    )(places, *token_sets, *decays, key_value)

    before = lax.ppermute(pair_state, "ctx", [(at, at + 2) for at in range(flips - 2)])
    for head in range(1, heads):
        own, other, _ = lax.optimization_barrier((query_own[head], query_sent[head], pair_state))
        parts.append(
            [xor_permute(other if flip % 2 else own, mesh, "ctx", flip) for flip in range(2, flips)]
        )

    returned = [[] for _ in SIDES]
    for head in range(heads):
        attended = pl.pallas_call(
            functools.partial(query_kernel, head, slice(head * size, (head + 1) * size), flips),
            in_specs=[SCALARS] + [VMEM] * (1 + flips + len(memory) + 1),
            out_specs=[VMEM] * sides,
            out_shape=[jax.ShapeDtypeStruct((rows, size), jnp.bfloat16)] * sides,
            scratch_shapes=[pltpu.VMEM((sides, pieces, size, size), jnp.bfloat16)],
            compiler_params=small,
            cost_estimate=pl.CostEstimate(
                flops=2 * sides * rows * size * (width + 4 * size),
                bytes_accessed=2 * (sides * rows * width + width * size),
                transcendentals=sides * rows * 4 * size,
            ),
            name="query",
        )(places, held, query_own[head], query_near, *parts[head], *memory, before)
        returned[0].append(attended[0])
        returned[1].append(xor_permute(attended[1], mesh, "ctx", 1))
        returned[2].append(xor_permute(attended[2], mesh, "groups", 1))
        returned[3].append(lax.ppermute(attended[3], ("groups", "ctx"), both))

    flat = [piece for side in returned for piece in side]
    return pl.pallas_call(
        functools.partial(merge_kernel, heads, size),
        in_specs=[SCALARS] + [VMEM] * len(flat),
        out_specs=VMEM,
        out_shape=jax.ShapeDtypeStruct((rows, heads_here * size), jnp.bfloat16),
        name="merge",
    )(places, *flat)


def spreads(mesh, tokens, query_weight, key_weight, value_weight, log_decay):
    sizes = tuple(mesh.shape[axis] for axis in ("groups", "ctx", "fsdp", "head"))
    if sizes != (2, 4, 2, 2):
        return False
    heads_here = log_decay.shape[0]
    depth = query_weight.shape[0]
    size = query_weight.shape[1] // heads_here
    return (
        heads_here % 4 == 0
        and size == PIECE
        and depth % 128 == 0
        and depth * 4 == tokens.shape[1]
        and tokens.shape[0] % PIECE == 0
        and tokens.shape[0] <= 512
    )


def local_body(mesh, *arrays):
    if spreads(mesh, *arrays):
        return spread_body(mesh, *arrays)
    return body(*arrays)


def solution(mesh):
    return jax.shard_map(
        functools.partial(local_body, mesh),
        mesh=mesh,
        in_specs=(
            P(("groups", "ctx"), None),
            P("ctx", ("fsdp", "head")),
            P("ctx", ("fsdp", "head")),
            P("ctx", ("fsdp", "head")),
            P(("fsdp", "head"), ("groups", "ctx")),
        ),
        out_specs=P(("groups", "ctx"), ("fsdp", "head")),
        check_vma=False,
    )
```

```python
import functools
import jax
import jax.numpy as jnp
from jax import lax
from jax.experimental import pallas as pl
from jax.experimental.pallas import tpu as pltpu
from jax.sharding import PartitionSpec as P

EPSILON = 1e-06


def prefix(shard, axis, join, neutral):
    place = lax.axis_index(axis)
    gathered = jax.tree.map(
        lambda a, kind: lax.all_gather(a.astype(kind), axis), shard, (jnp.bfloat16, jnp.bfloat16)
    )
    state = jax.tree.map(lambda a, e: jnp.zeros_like(a) + jnp.asarray(e, a.dtype), shard, neutral)

    def one(turn, state):
        return join(
            state,
            jax.tree.map(
                lambda a, own: lax.dynamic_index_in_dim(a, turn, 0, False).astype(own.dtype),
                gathered,
                shard,
            ),
        )

    return lax.fori_loop(0, place, one, state)


def row_folder(tokens):

    def accumulate(running, portions, offset):
        return tuple(
            (jnp.dot(tokens, portion, preferred_element_type=jnp.float32) for portion in portions)
        )

    return accumulate


def combine_states(earlier, later):
    return (earlier[0] + later[0], jnp.exp(later[0])[:, None, None] * earlier[1] + later[1])


def local_summary(key_rows, value_rows, cumulative):
    heads_here, row_count = cumulative.shape
    head_size = key_rows.shape[1] // heads_here
    to_end = jnp.exp(cumulative[:, -1:] - cumulative)
    scaled = (
        key_rows.reshape(row_count, heads_here, head_size).astype(jnp.float32)
        * to_end.T[:, :, None]
    ).astype(jnp.bfloat16)
    valueset = value_rows.reshape(row_count, heads_here, head_size)
    return jnp.einsum("khd,khe->hde", scaled, valueset, preferred_element_type=jnp.float32)


def carried(total_decay, own_state):
    identity = (jnp.zeros_like(total_decay), jnp.zeros_like(own_state))
    return prefix((total_decay, own_state), "ctx", combine_states, identity)


def attend(query_rows, key_rows, value_rows, cumulative, incoming):
    heads_here, row_count = cumulative.shape
    head_size = query_rows.shape[1] // heads_here
    block_rows = min(row_count, 512)
    queries = query_rows.reshape(row_count, heads_here, head_size)
    keyset = key_rows.reshape(row_count, heads_here, head_size)
    valueset = value_rows.reshape(row_count, heads_here, head_size)
    incoming_bf = incoming.astype(jnp.bfloat16)
    key_index = jnp.arange(row_count)

    def one_block(block_index):
        first_row = block_index * block_rows
        query_index = first_row + jnp.arange(block_rows)
        scores = jnp.einsum("qhd,khd->hqk", queries, keyset, preferred_element_type=jnp.float32)
        causal = key_index[None, :] <= query_index[:, None]
        decay_gaps = jnp.where(
            causal[None], cumulative[:, :, None] - cumulative[:, None, :], -jnp.inf
        )
        weights = (scores * jnp.exp(decay_gaps)).astype(jnp.bfloat16)
        within_part = jnp.einsum(
            "hqk,khe->qhe", weights, valueset, preferred_element_type=jnp.float32
        )
        carried_part = (
            jnp.einsum("qhd,hde->qhe", queries, incoming_bf, preferred_element_type=jnp.float32)
            * jnp.exp(cumulative).T[:, :, None]
        )
        raw_out = within_part + carried_part
        inverse_rms = lax.rsqrt(jnp.mean(raw_out * raw_out, axis=-1, keepdims=True) + EPSILON)
        return (raw_out * inverse_rms).astype(jnp.bfloat16)

    blocks = lax.map(one_block, jnp.arange(row_count // block_rows))
    return blocks.reshape(row_count, heads_here * head_size)


def body(tokens, query_weight, key_weight, value_weight, log_decay):
    row_count = tokens.shape[0]
    zero_rows = jnp.zeros((row_count, query_weight.shape[1]), jnp.float32)
    accumulate = row_folder(tokens)
    cumulative = jnp.cumsum(log_decay, axis=1)
    total_decay = cumulative[:, -1]
    query_sum, key_sum, value_sum = accumulate(
        (zero_rows, zero_rows, zero_rows),
        (
            lax.all_gather(query_weight, "ctx", axis=0, tiled=True),
            lax.all_gather(key_weight, "ctx", axis=0, tiled=True),
            lax.all_gather(value_weight, "ctx", axis=0, tiled=True),
        ),
        jnp.int32(0),
    )
    query_rows = jax.nn.silu(query_sum).astype(jnp.bfloat16)
    key_rows = jax.nn.silu(key_sum).astype(jnp.bfloat16)
    value_rows = value_sum.astype(jnp.bfloat16)
    incoming = carried(total_decay, local_summary(key_rows, value_rows, cumulative))[1]
    return attend(query_rows, key_rows, value_rows, cumulative, incoming)


SIDES = ("own", "ctx", "groups", "both")
PIECE = 128
ANY = pl.BlockSpec(memory_space=pl.ANY)
VMEM = pl.BlockSpec(memory_space=pltpu.VMEM)
SCALARS = pl.BlockSpec(memory_space=pltpu.SMEM)


def xor_permute(array, mesh, axis, flip):
    return lax.ppermute(array, axis, [(at, at ^ flip) for at in range(mesh.shape[axis])])


def after(arrays, *earlier):
    return lax.optimization_barrier((*arrays, *earlier))[: len(arrays)]


def in_three(array):
    parts = []
    for _ in range(3):
        part = lax.reduce_precision(array, 8, 7)
        parts.append(part.astype(jnp.bfloat16))
        array = array - part
    return jnp.concatenate(parts, axis=0)


def silu(rows):
    return rows / (1.0 + jnp.exp(-rows))


def running_sum(rows):
    lane = lax.broadcasted_iota(jnp.int32, rows.shape, 1)
    shift = 1
    while shift < rows.shape[1]:
        rows += jnp.where(lane >= shift, pltpu.roll(rows, shift, 1), 0.0)
        shift *= 2
    return rows


def column_of(row):
    return jnp.transpose(jnp.broadcast_to(row, (PIECE, row.shape[1])))


def token_copies(places, token_refs, held, semaphores):
    turn, share = places[0], places[1] * 2 + places[2]
    own_ref, quarter_refs = token_refs[0], token_refs[1:]
    width = held.shape[3]

    def copy(source, side, flip):
        return pltpu.make_async_copy(source, held.at[side, flip], semaphores.at[side, flip])

    def start():
        for side in range(len(SIDES)):
            for flip in range(held.shape[1]):
                block = turn ^ flip
                if side == 0:
                    at = pl.multiple_of(block * width, width)
                    copy(own_ref.at[:, pl.ds(at, width)], side, flip).start()
                    continue
                for place, ref in enumerate(quarter_refs[4 * (side - 1) : 4 * side]):

                    @pl.when(block ^ share == place)
                    def _(ref=ref):
                        copy(ref.at[0 : held.shape[2], :], side, flip).start()

    def wait(side):
        for flip in range(held.shape[1]):
            copy(quarter_refs[0].at[0 : held.shape[2], :], side, flip).wait()

    return start, wait


def project(held, side, cut, weights):
    total = None
    for flip, weight in enumerate(weights):
        product = jnp.dot(held[side, flip, cut, :], weight, preferred_element_type=jnp.float32)
        total = product if total is None else total + product
    return total


def piece_rows(rows):
    return [slice(at, at + PIECE) for at in range(0, rows, PIECE)]


def staggered(items, *stages):
    carried = {}
    for turn in range(len(items) + len(stages) - 1):
        for depth in reversed(range(len(stages))):
            at = turn - depth
            if 0 <= at < len(items):
                carried[at] = stages[depth](items[at], carried.get(at))


def key_value_kernel(head_here, heads_all, size, flips, places, *refs):
    heads = 1
    sides = len(SIDES)
    token_refs, refs = refs[:13], refs[13:]
    tail_ref, refs = refs[0], refs[1:]
    source_ref, key_ref, value_ref, state_ref, sum_ref, fade_ref, mask_ref, pair_ref, held = refs[:9]
    weight_ref, decay_ref, end_ref, tails, semaphores, weight_semaphores, tail_semaphores = refs[9:]
    tail_rows = pl.ds(held.shape[2], tails.shape[1])
    tail_loads = [
        pltpu.make_async_copy(source, tails.at[side], tail_semaphores.at[side])
        for side, source in enumerate([tail_ref, *(ref.at[tail_rows, :] for ref in token_refs[1::4])])
    ]
    for load in tail_loads:
        load.start()
    columns = pl.ds(2 * head_here * size, 2 * size)
    loads = [
        pltpu.make_async_copy(
            source_ref.at[places[0] ^ flip, :, columns], weight_ref.at[flip], weight_semaphores.at[flip]
        )
        for flip in range(flips)
    ]
    for load in loads:
        load.start()
    start, wait = token_copies(places, token_refs, held, semaphores)
    start()
    odd = places[0] % 2 == 1
    causal = lax.broadcasted_iota(jnp.int32, (PIECE, PIECE), 1) <= lax.broadcasted_iota(
        jnp.int32, (PIECE, PIECE), 0
    )
    cuts = piece_rows(key_ref.shape[1])
    for load in loads:
        load.wait()

    def decays(side):
        tail_loads[side].wait()
        part = tails[side].astype(jnp.float32)
        count = part.shape[0] // 3
        log_decay = part[:count] + (part[count : 2 * count] + part[2 * count :])
        decay_ref[...] = running_sum(log_decay[:, : sum_ref.shape[2]])
        for head in range(heads):
            row = decay_ref[pl.ds(places[3] * heads_all + head_here, 1), :]
            sum_ref[side, head : head + 1, :] = row
            column = column_of(row)
            begin = jnp.zeros_like(column[:1])
            for cut in cuts:
                end = column[cut.stop - 1 : cut.stop, :]
                end_ref[head, side, cut, :] = jnp.exp(end - column[cut])
                fade_ref[head, side, cut, :] = jnp.exp(column[cut] - begin)
                gaps = jnp.where(causal, column[cut] - row[:, cut], -jnp.inf)
                mask_ref[head, side, cut, :] = jnp.exp(gaps)
                begin = end

    def first(item, _):
        side, head, piece = item
        if piece == 0:
            wait(side)
            decays(side)
        at = slice(2 * head * size, 2 * (head + 1) * size)
        return project(held, side, cuts[piece], [weight_ref[flip, :, at] for flip in range(flips)])

    def second(item, both):
        side, head, piece = item
        cut, to = cuts[piece], slice(head * size, (head + 1) * size)
        key = silu(both[:, :size]).astype(jnp.bfloat16)
        value = both[:, size:].astype(jnp.bfloat16)
        key_ref[side, cut, to] = key
        value_ref[side, cut, to] = value
        scaled = (key.astype(jnp.float32) * end_ref[head, side, cut, :]).astype(jnp.bfloat16)
        return scaled, value

    def third(item, pair):
        side, head, piece = item
        state = lax.dot_general(
            pair[0], pair[1], (((0,), (0,)), ((), ())), preferred_element_type=jnp.float32
        )
        if piece:
            sums, cut = sum_ref[side, head : head + 1, :], cuts[piece]
            fade = sums[:, cut.stop - 1 : cut.stop] - sums[:, cut.start - 1 : cut.start]
            state += jnp.exp(fade) * state_ref[head, side, piece - 1]
        state_ref[head, side, piece] = state

    staggered(
        [(side, head, piece) for side in range(sides) for head in range(heads) for piece in range(len(cuts))],
        first,
        second,
        third,
    )
    last = len(cuts) - 1
    end = sum_ref.shape[2] - 1
    for head in range(heads):
        for pair in range(2):
            own, other = state_ref[head, 2 * pair, last], state_ref[head, 2 * pair + 1, last]
            own_total = sum_ref[2 * pair, head : head + 1, end:]
            other_total = sum_ref[2 * pair + 1, head : head + 1, end:]
            total = jnp.where(odd, own_total, other_total)
            first, second = jnp.where(odd, other, own), jnp.where(odd, own, other)
            pair_ref[head, pair] = (jnp.exp(total) * first + second).astype(jnp.bfloat16)


def query_kernel(head, columns, flips, places, *refs):
    sides = len(SIDES)
    token_refs, refs = refs[:13], refs[13:]
    weight_refs, refs = refs[:flips], refs[flips:]
    key_ref, value_ref, state_ref, sum_ref, fade_ref, mask_ref, before_ref = refs[:7]
    out_refs, (incoming_ref, held, semaphores) = refs[7:-3], refs[-3:]
    start, wait = token_copies(places, token_refs, held, semaphores)
    start()
    odd = places[0] % 2 == 1
    cuts = piece_rows(key_ref.shape[1])
    last = len(cuts) - 1
    end = sum_ref.shape[2] - 1
    at = slice(head * PIECE, (head + 1) * PIECE)
    weights = [ref[:, columns] if flip == 1 else ref[...] for flip, ref in enumerate(weight_refs)]
    for side in range(sides):
        partner = side ^ 1
        before = before_ref[head, side // 2].astype(jnp.float32)
        total = sum_ref[partner, head : head + 1, end:]
        later = jnp.exp(total) * before + state_ref[head, partner, last]
        second = odd if side % 2 == 0 else jnp.logical_not(odd)
        incoming = jnp.where(second, later, before)
        for piece, cut in enumerate(cuts):
            state = incoming
            if piece:
                sofar = jnp.exp(sum_ref[side, head : head + 1, cut.start - 1 : cut.start])
                state = state_ref[head, side, piece - 1] + sofar * incoming
            incoming_ref[side, piece] = state.astype(jnp.bfloat16)

    def first(item, _):
        side, piece = item
        if piece == 0:
            wait(side)
        return silu(project(held, side, cuts[piece], weights)).astype(jnp.bfloat16)

    def second(item, query):
        side, cut = item[0], cuts[item[1]]
        scores = lax.dot_general(
            query, key_ref[side, cut, at], (((1,), (1,)), ((), ())), preferred_element_type=jnp.float32
        )
        raw = jnp.dot(query, incoming_ref[side, item[1]], preferred_element_type=jnp.float32)
        return (scores * mask_ref[head, side, cut, :]).astype(jnp.bfloat16), raw * fade_ref[head, side, cut, :]

    def third(item, pair):
        side, cut = item[0], cuts[item[1]]
        return pair[1] + jnp.dot(pair[0], value_ref[side, cut, at], preferred_element_type=jnp.float32)

    def fourth(item, raw):
        side, cut = item[0], cuts[item[1]]
        scale = lax.rsqrt(jnp.mean(raw * raw, axis=1, keepdims=True) + EPSILON)
        out_refs[side][cut, :] = (raw * scale).astype(jnp.bfloat16)

    staggered(
        [(side, piece) for side in range(sides) for piece in range(len(cuts))], first, second, third, fourth
    )


def merge_kernel(heads, size, places, *refs):
    pieces, out_ref = refs[:-1], refs[-1]
    for side in range(len(SIDES)):
        for head in range(heads):
            at = pl.multiple_of(((places[3] ^ side) * heads + head) * size, size)
            out_ref[:, pl.ds(at, size)] = pieces[side * heads + head][...]


def pack_kernel(heads, size, places, *refs):
    out_ref = refs[4]
    for flip in range(out_ref.shape[0]):
        key_ref, value_ref = refs[2 * (flip % 2) : 2 * (flip % 2) + 2]
        for head in range(heads):
            at, to = head * size, 2 * head * size
            out_ref[places[0] ^ flip, :, to : to + size] = key_ref[:, at : at + size]
            out_ref[places[0] ^ flip, :, to + size : to + 2 * size] = value_ref[:, at : at + size]


def spread_body(mesh, tokens, query_weight, key_weight, value_weight, log_decay):
    rows, width = tokens.shape
    depth = query_weight.shape[0]
    heads_here = log_decay.shape[0]
    size = query_weight.shape[1] // heads_here
    flips = mesh.shape["ctx"]
    heads = heads_here // 4
    sides = len(SIDES)
    group, turn = lax.axis_index("groups"), lax.axis_index("ctx")
    plane, core = lax.axis_index("fsdp"), lax.axis_index("head")
    mine = group * 2 + turn % 2
    places = jnp.stack([turn, core, plane, mine]).astype(jnp.int32)
    both = [
        (at, (at // flips ^ 1) * flips + (at % flips ^ 1)) for at in range(mesh.shape["groups"] * flips)
    ]

    share = core * 2 + plane
    quarter = lax.dynamic_slice(tokens, (0, share * depth), (rows, depth))
    tail = jnp.pad(in_three(log_decay), ((0, 0), (0, depth - rows)))
    quarter = jnp.concatenate([quarter, tail], axis=0)

    steps = 2
    block = (depth // steps, heads * size)
    owners = pl.BlockSpec(block, lambda step, places: (step, places[3]))
    partners = pl.BlockSpec(block, lambda step, places: (step, places[3] ^ 1))
    packed_shape = (flips, depth, 2 * heads * size)
    packed = pl.pallas_call(
        functools.partial(pack_kernel, heads, size),
        grid_spec=pltpu.PrefetchScalarGridSpec(
            num_scalar_prefetch=1,
            grid=(steps,),
            in_specs=[owners, owners, partners, partners],
            out_specs=pl.BlockSpec((flips, depth // steps, 2 * heads * size), lambda step, places: (0, step, 0)),
        ),
        out_shape=jax.ShapeDtypeStruct(packed_shape, jnp.bfloat16),
        cost_estimate=pl.CostEstimate(flops=0, bytes_accessed=32 * depth * heads * size, transcendentals=0),
        name="pack",
    )(places, key_weight, value_weight, key_weight, value_weight)

    key_value = lax.all_to_all(packed, "ctx", 0, 0)

    from_ctx = xor_permute(quarter, mesh, "ctx", 1)
    from_groups = xor_permute(quarter, mesh, "groups", 1)
    (from_ctx,) = after((from_ctx,), from_groups)
    ctx_core = xor_permute(from_ctx, mesh, "head", 1)
    (from_ctx,) = after((from_ctx,), ctx_core)
    ctx_plane = xor_permute(from_ctx, mesh, "fsdp", 1)
    from_both = xor_permute(from_ctx, mesh, "groups", 1)
    beside = after((tokens,), from_ctx)[0]
    beside = lax.dynamic_slice(beside, (0, (share ^ 1) * depth), (rows, depth))
    groups_plane = xor_permute(beside, mesh, "groups", 1)
    both_core = xor_permute(from_both, mesh, "head", 1)
    (from_both,) = after((from_both,), both_core, ctx_plane)
    both_plane = xor_permute(from_both, mesh, "fsdp", 1)
    (both_plane,) = after((both_plane,), groups_plane)
    token_sets = [tokens]
    token_sets += [from_ctx, ctx_plane, ctx_core, xor_permute(ctx_plane, mesh, "head", 1)]
    for array in (from_groups, groups_plane):
        token_sets.append(array)
    token_sets += [xor_permute(array, mesh, "head", 1) for array in (from_groups, groups_plane)]
    token_sets += [from_both, both_plane, both_core, xor_permute(both_plane, mesh, "head", 1)]
    def query_block(owner, head, count):
        return lax.dynamic_slice(query_weight, (0, (owner * heads + head) * size), (depth, count * size))

    query_own = [query_block(mine, head, 1) for head in range(heads)]
    query_sent = [query_block(mine ^ 1, head, 1) for head in range(heads)]
    near_block, own, other = after(
        (query_block(mine ^ 1, 0, heads), query_own[0], query_sent[0]), both_plane
    )
    query_near = xor_permute(near_block, mesh, "ctx", 1)
    parts = [
        [xor_permute(other if flip % 2 else own, mesh, "ctx", flip) for flip in range(2, flips)]
    ]

    large, small = (pltpu.CompilerParams(vmem_limit_bytes=size << 20) for size in (38, 24))
    pieces = rows // PIECE
    column_shape = (sides, rows, size)
    shapes = [
        (column_shape, jnp.bfloat16),
        (column_shape, jnp.bfloat16),
        ((1, sides, pieces, size, size), jnp.float32),
        ((sides, 1, rows), jnp.float32),
        ((1, sides, rows, size), jnp.float32),
        ((1, sides, rows, size), jnp.float32),
        ((1, 2, size, size), jnp.bfloat16),
    ]
    held_shape = ((sides, flips, rows, depth), jnp.bfloat16)
    memory, before = [], []
    for head in range(heads):
        results = pl.pallas_call(
            functools.partial(key_value_kernel, head, heads, size, flips),
            in_specs=[SCALARS] + [ANY] * (len(token_sets) + 2),
            out_specs=[VMEM] * len(shapes),
            scratch_shapes=[
                pltpu.VMEM(*held_shape),
                pltpu.VMEM((flips, depth, 2 * size), jnp.bfloat16),
                pltpu.VMEM(log_decay.shape, jnp.float32),
                pltpu.VMEM((1, sides, rows, size), jnp.float32),
                pltpu.VMEM((sides, *tail.shape), jnp.bfloat16),
                pltpu.SemaphoreType.DMA((sides, flips)),
                pltpu.SemaphoreType.DMA((flips,)),
                pltpu.SemaphoreType.DMA((sides,)),
            ],
            out_shape=[jax.ShapeDtypeStruct(*shape) for shape in shapes],
            compiler_params=large,
            cost_estimate=pl.CostEstimate(
                flops=2 * sides * rows * width * 2 * size,
                bytes_accessed=2 * (sides * rows * width + width * 2 * size),
                transcendentals=sides * rows * 2 * size,
            ),
            name="key_value",
        )(places, *token_sets, tail, key_value)
        memory.append(results[:6])
        pair_state = results[6]
        before.append(lax.ppermute(pair_state, "ctx", [(at, at + 2) for at in range(flips - 2)]))
        if head + 1 < heads:
            own, other = after((query_own[head + 1], query_sent[head + 1]), pair_state, query_near)
            parts.append(
                [xor_permute(other if flip % 2 else own, mesh, "ctx", flip) for flip in range(2, flips)]
            )

    returned = [[] for _ in SIDES]
    for head in range(heads):
        attended = pl.pallas_call(
            functools.partial(query_kernel, 0, slice(head * size, (head + 1) * size), flips),
            in_specs=[SCALARS] + [ANY] * len(token_sets) + [VMEM] * (flips + 7),
            out_specs=[VMEM] * sides,
            out_shape=[jax.ShapeDtypeStruct((rows, size), jnp.bfloat16)] * sides,
            scratch_shapes=[
                pltpu.VMEM((sides, pieces, size, size), jnp.bfloat16),
                pltpu.VMEM(*held_shape),
                pltpu.SemaphoreType.DMA((sides, flips)),
            ],
            compiler_params=small,
            cost_estimate=pl.CostEstimate(
                flops=2 * sides * rows * size * (width + 4 * size),
                bytes_accessed=2 * (sides * rows * width + width * size),
                transcendentals=sides * rows * 4 * size,
            ),
            name="query",
        )(places, *token_sets, query_own[head], query_near, *parts[head], *memory[head], before[head])
        returned[0].append(attended[0])
        returned[1].append(xor_permute(attended[1], mesh, "ctx", 1))
        returned[2].append(xor_permute(attended[2], mesh, "groups", 1))
        returned[3].append(lax.ppermute(attended[3], ("groups", "ctx"), both))

    flat = [piece for side in returned for piece in side]
    return pl.pallas_call(
        functools.partial(merge_kernel, heads, size),
        in_specs=[SCALARS] + [VMEM] * len(flat),
        out_specs=VMEM,
        out_shape=jax.ShapeDtypeStruct((rows, heads_here * size), jnp.bfloat16),
        name="merge",
    )(places, *flat)


def spreads(mesh, tokens, query_weight, key_weight, value_weight, log_decay):
    sizes = tuple(mesh.shape[axis] for axis in ("groups", "ctx", "fsdp", "head"))
    if sizes != (2, 4, 2, 2):
        return False
    heads_here = log_decay.shape[0]
    depth = query_weight.shape[0]
    size = query_weight.shape[1] // heads_here
    return (
        heads_here % 4 == 0
        and size == PIECE
        and depth % 128 == 0
        and depth * 4 == tokens.shape[1]
        and tokens.shape[0] % PIECE == 0
        and tokens.shape[0] <= 512
    )


def local_body(mesh, *arrays):
    if spreads(mesh, *arrays):
        return spread_body(mesh, *arrays)
    return body(*arrays)


def solution(mesh):
    return jax.shard_map(
        functools.partial(local_body, mesh),
        mesh=mesh,
        in_specs=(
            P(("groups", "ctx"), None),
            P("ctx", ("fsdp", "head")),
            P("ctx", ("fsdp", "head")),
            P("ctx", ("fsdp", "head")),
            P(("fsdp", "head"), ("groups", "ctx")),
        ),
        out_specs=P(("groups", "ctx"), ("fsdp", "head")),
        check_vma=False,
    )
```

```python
import functools
import jax
import jax.numpy as jnp
from jax import lax
from jax.experimental import pallas as pl
from jax.experimental.pallas import tpu as pltpu
from jax.sharding import PartitionSpec as P

EPSILON = 1e-06


def prefix(shard, axis, join, neutral):
    place = lax.axis_index(axis)
    gathered = jax.tree.map(
        lambda a, kind: lax.all_gather(a.astype(kind), axis), shard, (jnp.bfloat16, jnp.bfloat16)
    )
    state = jax.tree.map(lambda a, e: jnp.zeros_like(a) + jnp.asarray(e, a.dtype), shard, neutral)

    def one(turn, state):
        return join(
            state,
            jax.tree.map(
                lambda a, own: lax.dynamic_index_in_dim(a, turn, 0, False).astype(own.dtype),
                gathered,
                shard,
            ),
        )

    return lax.fori_loop(0, place, one, state)


def row_folder(tokens):

    def accumulate(running, portions, offset):
        return tuple(
            (jnp.dot(tokens, portion, preferred_element_type=jnp.float32) for portion in portions)
        )

    return accumulate


def combine_states(earlier, later):
    return (earlier[0] + later[0], jnp.exp(later[0])[:, None, None] * earlier[1] + later[1])


def local_summary(key_rows, value_rows, cumulative):
    heads_here, row_count = cumulative.shape
    head_size = key_rows.shape[1] // heads_here
    to_end = jnp.exp(cumulative[:, -1:] - cumulative)
    scaled = (
        key_rows.reshape(row_count, heads_here, head_size).astype(jnp.float32)
        * to_end.T[:, :, None]
    ).astype(jnp.bfloat16)
    valueset = value_rows.reshape(row_count, heads_here, head_size)
    return jnp.einsum("khd,khe->hde", scaled, valueset, preferred_element_type=jnp.float32)


def carried(total_decay, own_state):
    identity = (jnp.zeros_like(total_decay), jnp.zeros_like(own_state))
    return prefix((total_decay, own_state), "ctx", combine_states, identity)


def attend(query_rows, key_rows, value_rows, cumulative, incoming):
    heads_here, row_count = cumulative.shape
    head_size = query_rows.shape[1] // heads_here
    block_rows = min(row_count, 512)
    queries = query_rows.reshape(row_count, heads_here, head_size)
    keyset = key_rows.reshape(row_count, heads_here, head_size)
    valueset = value_rows.reshape(row_count, heads_here, head_size)
    incoming_bf = incoming.astype(jnp.bfloat16)
    key_index = jnp.arange(row_count)

    def one_block(block_index):
        first_row = block_index * block_rows
        query_index = first_row + jnp.arange(block_rows)
        scores = jnp.einsum("qhd,khd->hqk", queries, keyset, preferred_element_type=jnp.float32)
        causal = key_index[None, :] <= query_index[:, None]
        decay_gaps = jnp.where(
            causal[None], cumulative[:, :, None] - cumulative[:, None, :], -jnp.inf
        )
        weights = (scores * jnp.exp(decay_gaps)).astype(jnp.bfloat16)
        within_part = jnp.einsum(
            "hqk,khe->qhe", weights, valueset, preferred_element_type=jnp.float32
        )
        carried_part = (
            jnp.einsum("qhd,hde->qhe", queries, incoming_bf, preferred_element_type=jnp.float32)
            * jnp.exp(cumulative).T[:, :, None]
        )
        raw_out = within_part + carried_part
        inverse_rms = lax.rsqrt(jnp.mean(raw_out * raw_out, axis=-1, keepdims=True) + EPSILON)
        return (raw_out * inverse_rms).astype(jnp.bfloat16)

    blocks = lax.map(one_block, jnp.arange(row_count // block_rows))
    return blocks.reshape(row_count, heads_here * head_size)


def body(tokens, query_weight, key_weight, value_weight, log_decay):
    row_count = tokens.shape[0]
    zero_rows = jnp.zeros((row_count, query_weight.shape[1]), jnp.float32)
    accumulate = row_folder(tokens)
    cumulative = jnp.cumsum(log_decay, axis=1)
    total_decay = cumulative[:, -1]
    query_sum, key_sum, value_sum = accumulate(
        (zero_rows, zero_rows, zero_rows),
        (
            lax.all_gather(query_weight, "ctx", axis=0, tiled=True),
            lax.all_gather(key_weight, "ctx", axis=0, tiled=True),
            lax.all_gather(value_weight, "ctx", axis=0, tiled=True),
        ),
        jnp.int32(0),
    )
    query_rows = jax.nn.silu(query_sum).astype(jnp.bfloat16)
    key_rows = jax.nn.silu(key_sum).astype(jnp.bfloat16)
    value_rows = value_sum.astype(jnp.bfloat16)
    incoming = carried(total_decay, local_summary(key_rows, value_rows, cumulative))[1]
    return attend(query_rows, key_rows, value_rows, cumulative, incoming)


SIDES = ("own", "ctx", "groups", "both")
PIECE = 128
ANY = pl.BlockSpec(memory_space=pl.ANY)
VMEM = pl.BlockSpec(memory_space=pltpu.VMEM)
SCALARS = pl.BlockSpec(memory_space=pltpu.SMEM)


def xor_permute(array, mesh, axis, flip):
    return lax.ppermute(array, axis, [(at, at ^ flip) for at in range(mesh.shape[axis])])


def after(arrays, *earlier):
    return lax.optimization_barrier((*arrays, *earlier))[: len(arrays)]


def in_three(array):
    parts = []
    for _ in range(3):
        part = lax.reduce_precision(array, 8, 7)
        parts.append(part.astype(jnp.bfloat16))
        array = array - part
    return jnp.concatenate(parts, axis=0)


def silu(rows):
    return rows / (1.0 + jnp.exp(-rows))


def running_sum(rows):
    lane = lax.broadcasted_iota(jnp.int32, rows.shape, 1)
    shift = 1
    while shift < rows.shape[1]:
        rows += jnp.where(lane >= shift, pltpu.roll(rows, shift, 1), 0.0)
        shift *= 2
    return rows


def column_of(row):
    return jnp.transpose(jnp.broadcast_to(row, (PIECE, row.shape[1])))


def token_copies(places, token_refs, held, semaphores, chosen=range(len(SIDES))):
    turn, share = places[0], places[1] * 2 + places[2]
    own_ref, quarter_refs = token_refs[0], token_refs[1:]
    width = held.shape[3]

    def copy(source, side, flip):
        return pltpu.make_async_copy(source, held.at[side, flip], semaphores.at[side, flip])

    def start():
        for side in chosen:
            for flip in range(held.shape[1]):
                block = turn ^ flip
                if side == 0:
                    at = pl.multiple_of(block * width, width)
                    copy(own_ref.at[:, pl.ds(at, width)], side, flip).start()
                    continue
                for place, ref in enumerate(quarter_refs[4 * (side - 1) : 4 * side]):

                    @pl.when(block ^ share == place)
                    def _(ref=ref):
                        copy(ref.at[0 : held.shape[2], :], side, flip).start()

    def wait(side):
        for flip in range(held.shape[1]):
            copy(quarter_refs[0].at[0 : held.shape[2], :], side, flip).wait()

    return start, wait


def project(held, side, cut, weights):
    total = None
    for flip, weight in enumerate(weights):
        product = jnp.dot(held[side, flip, cut, :], weight, preferred_element_type=jnp.float32)
        total = product if total is None else total + product
    return total


def piece_rows(rows):
    return [slice(at, at + PIECE) for at in range(0, rows, PIECE)]


def staggered(items, *stages):
    carried = {}
    for turn in range(len(items) + len(stages) - 1):
        for depth in reversed(range(len(stages))):
            at = turn - depth
            if 0 <= at < len(items):
                carried[at] = stages[depth](items[at], carried.get(at))


def key_value_kernel(head_here, heads_all, size, flips, places, *refs):
    heads = 1
    sides = len(SIDES)
    token_refs, refs = refs[:13], refs[13:]
    tail_ref, refs = refs[0], refs[1:]
    source_ref, key_ref, value_ref, state_ref, sum_ref, fade_ref, mask_ref, pair_ref, held = refs[:9]
    weight_ref, decay_ref, end_ref, tails, semaphores, weight_semaphores, tail_semaphores = refs[9:]
    tail_rows = pl.ds(held.shape[2], tails.shape[1])
    tail_loads = [
        pltpu.make_async_copy(source, tails.at[side], tail_semaphores.at[side])
        for side, source in enumerate([tail_ref, *(ref.at[tail_rows, :] for ref in token_refs[1::4])])
    ]
    for load in tail_loads:
        load.start()
    columns = pl.ds(2 * head_here * size, 2 * size)
    loads = [
        pltpu.make_async_copy(
            source_ref.at[places[0] ^ flip, :, columns], weight_ref.at[flip], weight_semaphores.at[flip]
        )
        for flip in range(flips)
    ]
    for load in loads:
        load.start()
    start, wait = token_copies(places, token_refs, held, semaphores)
    start()
    odd = places[0] % 2 == 1
    causal = lax.broadcasted_iota(jnp.int32, (PIECE, PIECE), 1) <= lax.broadcasted_iota(
        jnp.int32, (PIECE, PIECE), 0
    )
    cuts = piece_rows(key_ref.shape[1])
    for load in loads:
        load.wait()

    def decays(side):
        tail_loads[side].wait()
        part = tails[side].astype(jnp.float32)
        count = part.shape[0] // 3
        log_decay = part[:count] + (part[count : 2 * count] + part[2 * count :])
        decay_ref[...] = running_sum(log_decay[:, : sum_ref.shape[2]])
        for head in range(heads):
            row = decay_ref[pl.ds(places[3] * heads_all + head_here, 1), :]
            sum_ref[side, head : head + 1, :] = row
            column = column_of(row)
            begin = jnp.zeros_like(column[:1])
            for cut in cuts:
                end = column[cut.stop - 1 : cut.stop, :]
                end_ref[head, side, cut, :] = jnp.exp(end - column[cut])
                fade_ref[head, side, cut, :] = jnp.exp(column[cut] - begin)
                gaps = jnp.where(causal, column[cut] - row[:, cut], -jnp.inf)
                mask_ref[head, side, cut, :] = jnp.exp(gaps)
                begin = end

    def first(item, _):
        side, head, piece = item
        if piece == 0:
            wait(side)
            decays(side)
        at = slice(2 * head * size, 2 * (head + 1) * size)
        return project(held, side, cuts[piece], [weight_ref[flip, :, at] for flip in range(flips)])

    def second(item, both):
        side, head, piece = item
        cut, to = cuts[piece], slice(head * size, (head + 1) * size)
        key = silu(both[:, :size]).astype(jnp.bfloat16)
        value = both[:, size:].astype(jnp.bfloat16)
        key_ref[side, cut, to] = key
        value_ref[side, cut, to] = value
        scaled = (key.astype(jnp.float32) * end_ref[head, side, cut, :]).astype(jnp.bfloat16)
        return scaled, value

    def third(item, pair):
        side, head, piece = item
        state = lax.dot_general(
            pair[0], pair[1], (((0,), (0,)), ((), ())), preferred_element_type=jnp.float32
        )
        if piece:
            sums, cut = sum_ref[side, head : head + 1, :], cuts[piece]
            fade = sums[:, cut.stop - 1 : cut.stop] - sums[:, cut.start - 1 : cut.start]
            state += jnp.exp(fade) * state_ref[head, side, piece - 1]
        state_ref[head, side, piece] = state

    staggered(
        [(side, head, piece) for side in range(sides) for head in range(heads) for piece in range(len(cuts))],
        first,
        second,
        third,
    )
    last = len(cuts) - 1
    end = sum_ref.shape[2] - 1
    for head in range(heads):
        for pair in range(2):
            own, other = state_ref[head, 2 * pair, last], state_ref[head, 2 * pair + 1, last]
            own_total = sum_ref[2 * pair, head : head + 1, end:]
            other_total = sum_ref[2 * pair + 1, head : head + 1, end:]
            total = jnp.where(odd, own_total, other_total)
            first, second = jnp.where(odd, other, own), jnp.where(odd, own, other)
            pair_ref[head, pair] = (jnp.exp(total) * first + second).astype(jnp.bfloat16)


def query_kernel(chosen, head, columns, flips, places, *refs):
    token_refs, refs = refs[:13], refs[13:]
    weight_refs, refs = refs[:flips], refs[flips:]
    key_ref, value_ref, state_ref, sum_ref, fade_ref, mask_ref, before_ref = refs[:7]
    out_refs, (incoming_ref, held, semaphores) = refs[7:-3], refs[-3:]
    out_refs = dict(zip(chosen, out_refs))
    start, wait = token_copies(places, token_refs, held, semaphores, chosen)
    start()
    odd = places[0] % 2 == 1
    cuts = piece_rows(key_ref.shape[1])
    last = len(cuts) - 1
    end = sum_ref.shape[2] - 1
    at = slice(head * PIECE, (head + 1) * PIECE)
    weights = [ref[:, columns] if flip == 1 else ref[...] for flip, ref in enumerate(weight_refs)]
    for side in chosen:
        partner = side ^ 1
        before = before_ref[head, side // 2].astype(jnp.float32)
        total = sum_ref[partner, head : head + 1, end:]
        later = jnp.exp(total) * before + state_ref[head, partner, last]
        second = odd if side % 2 == 0 else jnp.logical_not(odd)
        incoming = jnp.where(second, later, before)
        for piece, cut in enumerate(cuts):
            state = incoming
            if piece:
                sofar = jnp.exp(sum_ref[side, head : head + 1, cut.start - 1 : cut.start])
                state = state_ref[head, side, piece - 1] + sofar * incoming
            incoming_ref[side, piece] = state.astype(jnp.bfloat16)

    def first(item, _):
        side, piece = item
        if piece == 0:
            wait(side)
        return silu(project(held, side, cuts[piece], weights)).astype(jnp.bfloat16)

    def second(item, query):
        side, cut = item[0], cuts[item[1]]
        scores = lax.dot_general(
            query, key_ref[side, cut, at], (((1,), (1,)), ((), ())), preferred_element_type=jnp.float32
        )
        raw = jnp.dot(query, incoming_ref[side, item[1]], preferred_element_type=jnp.float32)
        return (scores * mask_ref[head, side, cut, :]).astype(jnp.bfloat16), raw * fade_ref[head, side, cut, :]

    def third(item, pair):
        side, cut = item[0], cuts[item[1]]
        return pair[1] + jnp.dot(pair[0], value_ref[side, cut, at], preferred_element_type=jnp.float32)

    def fourth(item, raw):
        side, cut = item[0], cuts[item[1]]
        scale = lax.rsqrt(jnp.mean(raw * raw, axis=1, keepdims=True) + EPSILON)
        out_refs[side][cut, :] = (raw * scale).astype(jnp.bfloat16)

    staggered(
        [(side, piece) for side in chosen for piece in range(len(cuts))], first, second, third, fourth
    )


def merge_kernel(heads, size, places, *refs):
    pieces, out_ref = refs[:-1], refs[-1]
    for side in range(len(SIDES)):
        for head in range(heads):
            at = pl.multiple_of(((places[3] ^ side) * heads + head) * size, size)
            out_ref[:, pl.ds(at, size)] = pieces[side * heads + head][...]


def pack_kernel(heads, size, places, *refs):
    out_ref = refs[4]
    for flip in range(out_ref.shape[0]):
        key_ref, value_ref = refs[2 * (flip % 2) : 2 * (flip % 2) + 2]
        for head in range(heads):
            at, to = head * size, 2 * head * size
            out_ref[places[0] ^ flip, :, to : to + size] = key_ref[:, at : at + size]
            out_ref[places[0] ^ flip, :, to + size : to + 2 * size] = value_ref[:, at : at + size]


def spread_body(mesh, tokens, query_weight, key_weight, value_weight, log_decay):
    rows, width = tokens.shape
    depth = query_weight.shape[0]
    heads_here = log_decay.shape[0]
    size = query_weight.shape[1] // heads_here
    flips = mesh.shape["ctx"]
    heads = heads_here // 4
    sides = len(SIDES)
    group, turn = lax.axis_index("groups"), lax.axis_index("ctx")
    plane, core = lax.axis_index("fsdp"), lax.axis_index("head")
    mine = group * 2 + turn % 2
    places = jnp.stack([turn, core, plane, mine]).astype(jnp.int32)
    both = [
        (at, (at // flips ^ 1) * flips + (at % flips ^ 1)) for at in range(mesh.shape["groups"] * flips)
    ]

    share = core * 2 + plane
    quarter = lax.dynamic_slice(tokens, (0, share * depth), (rows, depth))
    tail = jnp.pad(in_three(log_decay), ((0, 0), (0, depth - rows)))
    quarter = jnp.concatenate([quarter, tail], axis=0)

    steps = 2
    block = (depth // steps, heads * size)
    owners = pl.BlockSpec(block, lambda step, places: (step, places[3]))
    partners = pl.BlockSpec(block, lambda step, places: (step, places[3] ^ 1))
    packed_shape = (flips, depth, 2 * heads * size)
    packed = pl.pallas_call(
        functools.partial(pack_kernel, heads, size),
        grid_spec=pltpu.PrefetchScalarGridSpec(
            num_scalar_prefetch=1,
            grid=(steps,),
            in_specs=[owners, owners, partners, partners],
            out_specs=pl.BlockSpec((flips, depth // steps, 2 * heads * size), lambda step, places: (0, step, 0)),
        ),
        out_shape=jax.ShapeDtypeStruct(packed_shape, jnp.bfloat16),
        cost_estimate=pl.CostEstimate(flops=0, bytes_accessed=32 * depth * heads * size, transcendentals=0),
        compiler_params=pltpu.CompilerParams(vmem_limit_bytes=16 << 20),
        name="pack",
    )(places, key_weight, value_weight, key_weight, value_weight)

    key_value = lax.all_to_all(packed, "ctx", 0, 0)

    from_ctx = xor_permute(quarter, mesh, "ctx", 1)
    from_groups = xor_permute(quarter, mesh, "groups", 1)
    ctx_core = xor_permute(from_ctx, mesh, "head", 1)
    (from_ctx,) = after((from_ctx,), ctx_core, from_groups)
    ctx_plane = xor_permute(from_ctx, mesh, "fsdp", 1)
    from_both = xor_permute(from_ctx, mesh, "groups", 1)
    beside = after((tokens,), from_ctx)[0]
    beside = lax.dynamic_slice(beside, (0, (share ^ 1) * depth), (rows, depth))
    groups_plane = xor_permute(beside, mesh, "groups", 1)
    both_core = xor_permute(from_both, mesh, "head", 1)
    (from_both,) = after((from_both,), both_core, ctx_plane)
    both_plane = xor_permute(from_both, mesh, "fsdp", 1)
    (both_plane,) = after((both_plane,), groups_plane)
    token_sets = [tokens]
    token_sets += [from_ctx, ctx_plane, ctx_core, xor_permute(ctx_plane, mesh, "head", 1)]
    for array in (from_groups, groups_plane):
        token_sets.append(array)
    token_sets += [xor_permute(array, mesh, "head", 1) for array in (from_groups, groups_plane)]
    token_sets += [from_both, both_plane, both_core, xor_permute(both_plane, mesh, "head", 1)]
    def query_block(owner, head, count):
        return lax.dynamic_slice(query_weight, (0, (owner * heads + head) * size), (depth, count * size))

    query_own = [query_block(mine, head, 1) for head in range(heads)]
    query_sent = [query_block(mine ^ 1, head, 1) for head in range(heads)]
    near_block, own, other = after(
        (query_block(mine ^ 1, 0, heads), query_own[0], query_sent[0]), from_both
    )
    query_near = xor_permute(near_block, mesh, "ctx", 1)
    parts = [
        [xor_permute(other if flip % 2 else own, mesh, "ctx", flip) for flip in range(2, flips)]
    ]

    large, small = (pltpu.CompilerParams(vmem_limit_bytes=size << 20) for size in (38, 24))
    pieces = rows // PIECE
    column_shape = (sides, rows, size)
    shapes = [
        (column_shape, jnp.bfloat16),
        (column_shape, jnp.bfloat16),
        ((1, sides, pieces, size, size), jnp.float32),
        ((sides, 1, rows), jnp.float32),
        ((1, sides, rows, size), jnp.float32),
        ((1, sides, rows, size), jnp.float32),
        ((1, 2, size, size), jnp.bfloat16),
    ]
    held_shape = ((sides, flips, rows, depth), jnp.bfloat16)
    memory, before = [], []
    for head in range(heads):
        results = pl.pallas_call(
            functools.partial(key_value_kernel, head, heads, size, flips),
            in_specs=[SCALARS] + [ANY] * (len(token_sets) + 2),
            out_specs=[VMEM] * len(shapes),
            scratch_shapes=[
                pltpu.VMEM(*held_shape),
                pltpu.VMEM((flips, depth, 2 * size), jnp.bfloat16),
                pltpu.VMEM(log_decay.shape, jnp.float32),
                pltpu.VMEM((1, sides, rows, size), jnp.float32),
                pltpu.VMEM((sides, *tail.shape), jnp.bfloat16),
                pltpu.SemaphoreType.DMA((sides, flips)),
                pltpu.SemaphoreType.DMA((flips,)),
                pltpu.SemaphoreType.DMA((sides,)),
            ],
            out_shape=[jax.ShapeDtypeStruct(*shape) for shape in shapes],
            compiler_params=large,
            cost_estimate=pl.CostEstimate(
                flops=2 * sides * rows * width * 2 * size,
                bytes_accessed=2 * (sides * rows * width + width * 2 * size),
                transcendentals=sides * rows * 2 * size,
            ),
            name="key_value",
        )(places, *token_sets, tail, key_value)
        memory.append(results[:6])
        pair_state = results[6]
        before.append(lax.ppermute(pair_state, "ctx", [(at, at + 2) for at in range(flips - 2)]))
        if head + 1 < heads:
            own, other = after((query_own[head + 1], query_sent[head + 1]), pair_state, query_near)
            parts.append(
                [xor_permute(other if flip % 2 else own, mesh, "ctx", flip) for flip in range(2, flips)]
            )

    def query(head, chosen, *gate):
        own = after((query_own[head],), *gate)[0] if gate else query_own[head]
        count = len(chosen)
        return pl.pallas_call(
            functools.partial(query_kernel, chosen, 0, slice(head * size, (head + 1) * size), flips),
            in_specs=[SCALARS] + [ANY] * len(token_sets) + [VMEM] * (flips + 7),
            out_specs=[VMEM] * count,
            out_shape=[jax.ShapeDtypeStruct((rows, size), jnp.bfloat16)] * count,
            scratch_shapes=[
                pltpu.VMEM((sides, pieces, size, size), jnp.bfloat16),
                pltpu.VMEM(*held_shape),
                pltpu.SemaphoreType.DMA((sides, flips)),
            ],
            compiler_params=small,
            cost_estimate=pl.CostEstimate(
                flops=2 * count * rows * size * (width + 4 * size),
                bytes_accessed=2 * (count * rows * width + width * size),
                transcendentals=count * rows * 4 * size,
            ),
            name="query",
        )(places, *token_sets, own, query_near, *parts[head], *memory[head], before[head])

    returned = [[] for _ in SIDES]
    for head in range(heads):
        if head < heads - 1:
            attended = query(head, tuple(range(sides)))
        else:
            away = query(head, tuple(range(1, sides)))
            attended = [*query(head, (0,), away[0]), *away]
        returned[0].append(attended[0])
        returned[1].append(xor_permute(attended[1], mesh, "ctx", 1))
        returned[2].append(xor_permute(attended[2], mesh, "groups", 1))
        returned[3].append(lax.ppermute(attended[3], ("groups", "ctx"), both))

    flat = [piece for side in returned for piece in side]
    return pl.pallas_call(
        functools.partial(merge_kernel, heads, size),
        in_specs=[SCALARS] + [VMEM] * len(flat),
        out_specs=VMEM,
        out_shape=jax.ShapeDtypeStruct((rows, heads_here * size), jnp.bfloat16),
        compiler_params=pltpu.CompilerParams(vmem_limit_bytes=8 << 20),
        name="merge",
    )(places, *flat)


def spreads(mesh, tokens, query_weight, key_weight, value_weight, log_decay):
    sizes = tuple(mesh.shape[axis] for axis in ("groups", "ctx", "fsdp", "head"))
    if sizes != (2, 4, 2, 2):
        return False
    heads_here = log_decay.shape[0]
    depth = query_weight.shape[0]
    size = query_weight.shape[1] // heads_here
    return (
        heads_here % 4 == 0
        and size == PIECE
        and depth % 128 == 0
        and depth * 4 == tokens.shape[1]
        and tokens.shape[0] % PIECE == 0
        and tokens.shape[0] <= 512
    )


def local_body(mesh, *arrays):
    if spreads(mesh, *arrays):
        return spread_body(mesh, *arrays)
    return body(*arrays)


def solution(mesh):
    return jax.shard_map(
        functools.partial(local_body, mesh),
        mesh=mesh,
        in_specs=(
            P(("groups", "ctx"), None),
            P("ctx", ("fsdp", "head")),
            P("ctx", ("fsdp", "head")),
            P("ctx", ("fsdp", "head")),
            P(("fsdp", "head"), ("groups", "ctx")),
        ),
        out_specs=P(("groups", "ctx"), ("fsdp", "head")),
        check_vma=False,
    )
```

```python
import functools
import jax
import jax.numpy as jnp
from jax import lax
from jax.experimental import pallas as pl
from jax.experimental.pallas import tpu as pltpu
from jax.sharding import PartitionSpec as P

EPSILON = 1e-06


def prefix(shard, axis, join, neutral):
    place = lax.axis_index(axis)
    gathered = jax.tree.map(
        lambda a, kind: lax.all_gather(a.astype(kind), axis), shard, (jnp.bfloat16, jnp.bfloat16)
    )
    state = jax.tree.map(lambda a, e: jnp.zeros_like(a) + jnp.asarray(e, a.dtype), shard, neutral)

    def one(turn, state):
        return join(
            state,
            jax.tree.map(
                lambda a, own: lax.dynamic_index_in_dim(a, turn, 0, False).astype(own.dtype),
                gathered,
                shard,
            ),
        )

    return lax.fori_loop(0, place, one, state)


def row_folder(tokens):

    def accumulate(running, portions, offset):
        return tuple(
            (jnp.dot(tokens, portion, preferred_element_type=jnp.float32) for portion in portions)
        )

    return accumulate


def combine_states(earlier, later):
    return (earlier[0] + later[0], jnp.exp(later[0])[:, None, None] * earlier[1] + later[1])


def local_summary(key_rows, value_rows, cumulative):
    heads_here, row_count = cumulative.shape
    head_size = key_rows.shape[1] // heads_here
    to_end = jnp.exp(cumulative[:, -1:] - cumulative)
    scaled = (
        key_rows.reshape(row_count, heads_here, head_size).astype(jnp.float32)
        * to_end.T[:, :, None]
    ).astype(jnp.bfloat16)
    valueset = value_rows.reshape(row_count, heads_here, head_size)
    return jnp.einsum("khd,khe->hde", scaled, valueset, preferred_element_type=jnp.float32)


def carried(total_decay, own_state):
    identity = (jnp.zeros_like(total_decay), jnp.zeros_like(own_state))
    return prefix((total_decay, own_state), "ctx", combine_states, identity)


def attend(query_rows, key_rows, value_rows, cumulative, incoming):
    heads_here, row_count = cumulative.shape
    head_size = query_rows.shape[1] // heads_here
    block_rows = min(row_count, 512)
    queries = query_rows.reshape(row_count, heads_here, head_size)
    keyset = key_rows.reshape(row_count, heads_here, head_size)
    valueset = value_rows.reshape(row_count, heads_here, head_size)
    incoming_bf = incoming.astype(jnp.bfloat16)
    key_index = jnp.arange(row_count)

    def one_block(block_index):
        first_row = block_index * block_rows
        query_index = first_row + jnp.arange(block_rows)
        scores = jnp.einsum("qhd,khd->hqk", queries, keyset, preferred_element_type=jnp.float32)
        causal = key_index[None, :] <= query_index[:, None]
        decay_gaps = jnp.where(
            causal[None], cumulative[:, :, None] - cumulative[:, None, :], -jnp.inf
        )
        weights = (scores * jnp.exp(decay_gaps)).astype(jnp.bfloat16)
        within_part = jnp.einsum(
            "hqk,khe->qhe", weights, valueset, preferred_element_type=jnp.float32
        )
        carried_part = (
            jnp.einsum("qhd,hde->qhe", queries, incoming_bf, preferred_element_type=jnp.float32)
            * jnp.exp(cumulative).T[:, :, None]
        )
        raw_out = within_part + carried_part
        inverse_rms = lax.rsqrt(jnp.mean(raw_out * raw_out, axis=-1, keepdims=True) + EPSILON)
        return (raw_out * inverse_rms).astype(jnp.bfloat16)

    blocks = lax.map(one_block, jnp.arange(row_count // block_rows))
    return blocks.reshape(row_count, heads_here * head_size)


def body(tokens, query_weight, key_weight, value_weight, log_decay):
    row_count = tokens.shape[0]
    zero_rows = jnp.zeros((row_count, query_weight.shape[1]), jnp.float32)
    accumulate = row_folder(tokens)
    cumulative = jnp.cumsum(log_decay, axis=1)
    total_decay = cumulative[:, -1]
    query_sum, key_sum, value_sum = accumulate(
        (zero_rows, zero_rows, zero_rows),
        (
            lax.all_gather(query_weight, "ctx", axis=0, tiled=True),
            lax.all_gather(key_weight, "ctx", axis=0, tiled=True),
            lax.all_gather(value_weight, "ctx", axis=0, tiled=True),
        ),
        jnp.int32(0),
    )
    query_rows = jax.nn.silu(query_sum).astype(jnp.bfloat16)
    key_rows = jax.nn.silu(key_sum).astype(jnp.bfloat16)
    value_rows = value_sum.astype(jnp.bfloat16)
    incoming = carried(total_decay, local_summary(key_rows, value_rows, cumulative))[1]
    return attend(query_rows, key_rows, value_rows, cumulative, incoming)


SIDES = ("own", "ctx", "groups", "both")
PIECE = 128
ANY = pl.BlockSpec(memory_space=pl.ANY)
VMEM = pl.BlockSpec(memory_space=pltpu.VMEM)
SCALARS = pl.BlockSpec(memory_space=pltpu.SMEM)


def xor_permute(array, mesh, axis, flip):
    return lax.ppermute(array, axis, [(at, at ^ flip) for at in range(mesh.shape[axis])])


def after(arrays, *earlier):
    return lax.optimization_barrier((*arrays, *earlier))[: len(arrays)]


def in_three(array):
    parts = []
    for _ in range(3):
        part = lax.reduce_precision(array, 8, 7)
        parts.append(part.astype(jnp.bfloat16))
        array = array - part
    return jnp.concatenate(parts, axis=0)


def silu(rows):
    return rows / (1.0 + jnp.exp(-rows))


def running_sum(rows):
    lane = lax.broadcasted_iota(jnp.int32, rows.shape, 1)
    shift = 1
    while shift < rows.shape[1]:
        rows += jnp.where(lane >= shift, pltpu.roll(rows, shift, 1), 0.0)
        shift *= 2
    return rows


def column_of(row):
    return jnp.transpose(jnp.broadcast_to(row, (PIECE, row.shape[1])))


def token_copies(places, token_refs, held, semaphores, chosen=range(len(SIDES))):
    turn, share = places[0], places[1] * 2 + places[2]
    own_ref, quarter_refs = token_refs[0], token_refs[1:]
    width = held.shape[3]

    def copy(source, side, flip):
        return pltpu.make_async_copy(source, held.at[side, flip], semaphores.at[side, flip])

    def start():
        for side in chosen:
            for flip in range(held.shape[1]):
                block = turn ^ flip
                if side == 0:
                    at = pl.multiple_of(block * width, width)
                    copy(own_ref.at[:, pl.ds(at, width)], side, flip).start()
                    continue
                for place, ref in enumerate(quarter_refs[4 * (side - 1) : 4 * side]):

                    @pl.when(block ^ share == place)
                    def _(ref=ref):
                        copy(ref.at[0 : held.shape[2], :], side, flip).start()

    def wait(side):
        for flip in range(held.shape[1]):
            copy(quarter_refs[0].at[0 : held.shape[2], :], side, flip).wait()

    return start, wait


def project(held, side, cut, weights):
    total = None
    for flip, weight in enumerate(weights):
        product = jnp.dot(held[side, flip, cut, :], weight, preferred_element_type=jnp.float32)
        total = product if total is None else total + product
    return total


def piece_rows(rows):
    return [slice(at, at + PIECE) for at in range(0, rows, PIECE)]


def staggered(items, *stages):
    carried = {}
    for turn in range(len(items) + len(stages) - 1):
        for depth in reversed(range(len(stages))):
            at = turn - depth
            if 0 <= at < len(items):
                carried[at] = stages[depth](items[at], carried.get(at))


def key_value_kernel(head_here, heads_all, size, flips, places, *refs):
    heads = 1
    sides = len(SIDES)
    token_refs, refs = refs[:13], refs[13:]
    tail_ref, refs = refs[0], refs[1:]
    source_ref, key_ref, value_ref, state_ref, sum_ref, fade_ref, mask_ref, pair_ref, held = refs[:9]
    weight_ref, decay_ref, end_ref, tails, semaphores, weight_semaphores, tail_semaphores = refs[9:]
    tail_rows = pl.ds(held.shape[2], tails.shape[1])
    tail_loads = [
        pltpu.make_async_copy(source, tails.at[side], tail_semaphores.at[side])
        for side, source in enumerate([tail_ref, *(ref.at[tail_rows, :] for ref in token_refs[1::4])])
    ]
    for load in tail_loads:
        load.start()
    columns = pl.ds(2 * head_here * size, 2 * size)
    loads = [
        pltpu.make_async_copy(
            source_ref.at[places[0] ^ flip, :, columns], weight_ref.at[flip], weight_semaphores.at[flip]
        )
        for flip in range(flips)
    ]
    for load in loads:
        load.start()
    start, wait = token_copies(places, token_refs, held, semaphores)
    start()
    odd = places[0] % 2 == 1
    causal = lax.broadcasted_iota(jnp.int32, (PIECE, PIECE), 1) <= lax.broadcasted_iota(
        jnp.int32, (PIECE, PIECE), 0
    )
    cuts = piece_rows(key_ref.shape[1])
    for load in loads:
        load.wait()

    def decays(side):
        tail_loads[side].wait()
        part = tails[side].astype(jnp.float32)
        count = part.shape[0] // 3
        log_decay = part[:count] + (part[count : 2 * count] + part[2 * count :])
        decay_ref[...] = running_sum(log_decay[:, : sum_ref.shape[2]])
        for head in range(heads):
            row = decay_ref[pl.ds(places[3] * heads_all + head_here, 1), :]
            sum_ref[side, head : head + 1, :] = row
            column = column_of(row)
            begin = jnp.zeros_like(column[:1])
            for cut in cuts:
                end = column[cut.stop - 1 : cut.stop, :]
                end_ref[head, side, cut, :] = jnp.exp(end - column[cut])
                fade_ref[head, side, cut, :] = jnp.exp(column[cut] - begin)
                gaps = jnp.where(causal, column[cut] - row[:, cut], -jnp.inf)
                mask_ref[head, side, cut, :] = jnp.exp(gaps)
                begin = end

    def first(item, _):
        side, head, piece = item
        if piece == 0:
            wait(side)
            decays(side)
        at = slice(2 * head * size, 2 * (head + 1) * size)
        return project(held, side, cuts[piece], [weight_ref[flip, :, at] for flip in range(flips)])

    def second(item, both):
        side, head, piece = item
        cut, to = cuts[piece], slice(head * size, (head + 1) * size)
        key = silu(both[:, :size]).astype(jnp.bfloat16)
        value = both[:, size:].astype(jnp.bfloat16)
        key_ref[side, cut, to] = key
        value_ref[side, cut, to] = value
        scaled = (key.astype(jnp.float32) * end_ref[head, side, cut, :]).astype(jnp.bfloat16)
        return scaled, value

    def third(item, pair):
        side, head, piece = item
        state = lax.dot_general(
            pair[0], pair[1], (((0,), (0,)), ((), ())), preferred_element_type=jnp.float32
        )
        if piece:
            sums, cut = sum_ref[side, head : head + 1, :], cuts[piece]
            fade = sums[:, cut.stop - 1 : cut.stop] - sums[:, cut.start - 1 : cut.start]
            state += jnp.exp(fade) * state_ref[head, side, piece - 1]
        state_ref[head, side, piece] = state

    staggered(
        [(side, head, piece) for side in range(sides) for head in range(heads) for piece in range(len(cuts))],
        first,
        second,
        third,
    )
    last = len(cuts) - 1
    end = sum_ref.shape[2] - 1
    for head in range(heads):
        for pair in range(2):
            own, other = state_ref[head, 2 * pair, last], state_ref[head, 2 * pair + 1, last]
            own_total = sum_ref[2 * pair, head : head + 1, end:]
            other_total = sum_ref[2 * pair + 1, head : head + 1, end:]
            total = jnp.where(odd, own_total, other_total)
            first, second = jnp.where(odd, other, own), jnp.where(odd, own, other)
            pair_ref[head, pair] = (jnp.exp(total) * first + second).astype(jnp.bfloat16)


def query_kernel(chosen, head, columns, flips, places, *refs):
    token_refs, refs = refs[:13], refs[13:]
    weight_refs, refs = refs[:flips], refs[flips:]
    key_ref, value_ref, state_ref, sum_ref, fade_ref, mask_ref, before_ref = refs[:7]
    out_refs, (incoming_ref, held, semaphores) = refs[7:-3], refs[-3:]
    out_refs = dict(zip(chosen, out_refs))
    start, wait = token_copies(places, token_refs, held, semaphores, chosen)
    start()
    odd = places[0] % 2 == 1
    cuts = piece_rows(key_ref.shape[1])
    last = len(cuts) - 1
    end = sum_ref.shape[2] - 1
    at = slice(head * PIECE, (head + 1) * PIECE)
    weights = [ref[:, columns] if flip == 1 else ref[...] for flip, ref in enumerate(weight_refs)]
    for side in chosen:
        partner = side ^ 1
        before = before_ref[head, side // 2].astype(jnp.float32)
        total = sum_ref[partner, head : head + 1, end:]
        later = jnp.exp(total) * before + state_ref[head, partner, last]
        second = odd if side % 2 == 0 else jnp.logical_not(odd)
        incoming = jnp.where(second, later, before)
        for piece, cut in enumerate(cuts):
            state = incoming
            if piece:
                sofar = jnp.exp(sum_ref[side, head : head + 1, cut.start - 1 : cut.start])
                state = state_ref[head, side, piece - 1] + sofar * incoming
            incoming_ref[side, piece] = state.astype(jnp.bfloat16)

    def first(item, _):
        side, piece = item
        if piece == 0:
            wait(side)
        return silu(project(held, side, cuts[piece], weights)).astype(jnp.bfloat16)

    def second(item, query):
        side, cut = item[0], cuts[item[1]]
        scores = lax.dot_general(
            query, key_ref[side, cut, at], (((1,), (1,)), ((), ())), preferred_element_type=jnp.float32
        )
        raw = jnp.dot(query, incoming_ref[side, item[1]], preferred_element_type=jnp.float32)
        return (scores * mask_ref[head, side, cut, :]).astype(jnp.bfloat16), raw * fade_ref[head, side, cut, :]

    def third(item, pair):
        side, cut = item[0], cuts[item[1]]
        return pair[1] + jnp.dot(pair[0], value_ref[side, cut, at], preferred_element_type=jnp.float32)

    def fourth(item, raw):
        side, cut = item[0], cuts[item[1]]
        scale = lax.rsqrt(jnp.mean(raw * raw, axis=1, keepdims=True) + EPSILON)
        out_refs[side][cut, :] = (raw * scale).astype(jnp.bfloat16)

    staggered(
        [(side, piece) for side in chosen for piece in range(len(cuts))], first, second, third, fourth
    )


def merge_kernel(heads, size, places, *refs):
    pieces, out_ref = refs[:-1], refs[-1]
    for side in range(len(SIDES)):
        for head in range(heads):
            at = pl.multiple_of(((places[3] ^ side) * heads + head) * size, size)
            out_ref[:, pl.ds(at, size)] = pieces[side * heads + head][...]


def pack_kernel(heads, size, places, *refs):
    out_ref = refs[4]
    for flip in range(out_ref.shape[0]):
        key_ref, value_ref = refs[2 * (flip % 2) : 2 * (flip % 2) + 2]
        for head in range(heads):
            at, to = head * size, 2 * head * size
            out_ref[places[0] ^ flip, :, to : to + size] = key_ref[:, at : at + size]
            out_ref[places[0] ^ flip, :, to + size : to + 2 * size] = value_ref[:, at : at + size]


def spread_body(mesh, tokens, query_weight, key_weight, value_weight, log_decay):
    rows, width = tokens.shape
    depth = query_weight.shape[0]
    heads_here = log_decay.shape[0]
    size = query_weight.shape[1] // heads_here
    flips = mesh.shape["ctx"]
    heads = heads_here // 4
    sides = len(SIDES)
    group, turn = lax.axis_index("groups"), lax.axis_index("ctx")
    plane, core = lax.axis_index("fsdp"), lax.axis_index("head")
    mine = group * 2 + turn % 2
    places = jnp.stack([turn, core, plane, mine]).astype(jnp.int32)
    both = [
        (at, (at // flips ^ 1) * flips + (at % flips ^ 1)) for at in range(mesh.shape["groups"] * flips)
    ]

    share = core * 2 + plane
    quarter = lax.dynamic_slice(tokens, (0, share * depth), (rows, depth))
    tail = jnp.pad(in_three(log_decay), ((0, 0), (0, depth - rows)))
    quarter = jnp.concatenate([quarter, tail], axis=0)

    steps = 2
    block = (depth // steps, heads * size)
    owners = pl.BlockSpec(block, lambda step, places: (step, places[3]))
    partners = pl.BlockSpec(block, lambda step, places: (step, places[3] ^ 1))
    packed_shape = (flips, depth, 2 * heads * size)
    packed = pl.pallas_call(
        functools.partial(pack_kernel, heads, size),
        grid_spec=pltpu.PrefetchScalarGridSpec(
            num_scalar_prefetch=1,
            grid=(steps,),
            in_specs=[owners, owners, partners, partners],
            out_specs=pl.BlockSpec((flips, depth // steps, 2 * heads * size), lambda step, places: (0, step, 0)),
        ),
        out_shape=jax.ShapeDtypeStruct(packed_shape, jnp.bfloat16),
        cost_estimate=pl.CostEstimate(flops=0, bytes_accessed=32 * depth * heads * size, transcendentals=0),
        name="pack",
    )(places, key_weight, value_weight, key_weight, value_weight)

    key_value = lax.all_to_all(packed, "ctx", 0, 0)

    from_ctx = xor_permute(quarter, mesh, "ctx", 1)
    from_groups = xor_permute(quarter, mesh, "groups", 1)
    ctx_core = xor_permute(from_ctx, mesh, "head", 1)
    (from_ctx,) = after((from_ctx,), ctx_core, from_groups)
    ctx_plane = xor_permute(from_ctx, mesh, "fsdp", 1)
    from_both = xor_permute(from_ctx, mesh, "groups", 1)
    beside = after((tokens,), from_ctx)[0]
    beside = lax.dynamic_slice(beside, (0, (share ^ 1) * depth), (rows, depth))
    groups_plane = xor_permute(beside, mesh, "groups", 1)
    both_core = xor_permute(from_both, mesh, "head", 1)
    (from_both,) = after((from_both,), both_core, ctx_plane)
    both_plane = xor_permute(from_both, mesh, "fsdp", 1)
    (both_plane,) = after((both_plane,), groups_plane)
    token_sets = [tokens]
    token_sets += [from_ctx, ctx_plane, ctx_core, xor_permute(ctx_plane, mesh, "head", 1)]
    for array in (from_groups, groups_plane):
        token_sets.append(array)
    token_sets += [xor_permute(array, mesh, "head", 1) for array in (from_groups, groups_plane)]
    token_sets += [from_both, both_plane, both_core, xor_permute(both_plane, mesh, "head", 1)]
    def query_block(owner, head, count):
        return lax.dynamic_slice(query_weight, (0, (owner * heads + head) * size), (depth, count * size))

    query_own = [query_block(mine, head, 1) for head in range(heads)]
    query_sent = [query_block(mine ^ 1, head, 1) for head in range(heads)]
    near_block, own, other = after(
        (query_block(mine ^ 1, 0, heads), query_own[0], query_sent[0]), from_both
    )
    query_near = xor_permute(near_block, mesh, "ctx", 1)
    parts = [
        [xor_permute(other if flip % 2 else own, mesh, "ctx", flip) for flip in range(2, flips)]
    ]

    large, small = (pltpu.CompilerParams(vmem_limit_bytes=size << 20) for size in (38, 24))
    pieces = rows // PIECE
    column_shape = (sides, rows, size)
    shapes = [
        (column_shape, jnp.bfloat16),
        (column_shape, jnp.bfloat16),
        ((1, sides, pieces, size, size), jnp.float32),
        ((sides, 1, rows), jnp.float32),
        ((1, sides, rows, size), jnp.float32),
        ((1, sides, rows, size), jnp.float32),
        ((1, 2, size, size), jnp.bfloat16),
    ]
    held_shape = ((sides, flips, rows, depth), jnp.bfloat16)
    memory, before = [], []
    for head in range(heads):
        results = pl.pallas_call(
            functools.partial(key_value_kernel, head, heads, size, flips),
            in_specs=[SCALARS] + [ANY] * (len(token_sets) + 2),
            out_specs=[VMEM] * len(shapes),
            scratch_shapes=[
                pltpu.VMEM(*held_shape),
                pltpu.VMEM((flips, depth, 2 * size), jnp.bfloat16),
                pltpu.VMEM(log_decay.shape, jnp.float32),
                pltpu.VMEM((1, sides, rows, size), jnp.float32),
                pltpu.VMEM((sides, *tail.shape), jnp.bfloat16),
                pltpu.SemaphoreType.DMA((sides, flips)),
                pltpu.SemaphoreType.DMA((flips,)),
                pltpu.SemaphoreType.DMA((sides,)),
            ],
            out_shape=[jax.ShapeDtypeStruct(*shape) for shape in shapes],
            compiler_params=large,
            cost_estimate=pl.CostEstimate(
                flops=2 * sides * rows * width * 2 * size,
                bytes_accessed=2 * (sides * rows * width + width * 2 * size),
                transcendentals=sides * rows * 2 * size,
            ),
            name="key_value",
        )(places, *token_sets, tail, key_value)
        memory.append(results[:6])
        pair_state = results[6]
        before.append(lax.ppermute(pair_state, "ctx", [(at, at + 2) for at in range(flips - 2)]))
        if head + 1 < heads:
            own, other = after((query_own[head + 1], query_sent[head + 1]), pair_state, query_near)
            parts.append(
                [xor_permute(other if flip % 2 else own, mesh, "ctx", flip) for flip in range(2, flips)]
            )

    def query(head, chosen, *gate):
        own = after((query_own[head],), *gate)[0] if gate else query_own[head]
        count = len(chosen)
        return pl.pallas_call(
            functools.partial(query_kernel, chosen, 0, slice(head * size, (head + 1) * size), flips),
            in_specs=[SCALARS] + [ANY] * len(token_sets) + [VMEM] * (flips + 7),
            out_specs=[VMEM] * count,
            out_shape=[jax.ShapeDtypeStruct((rows, size), jnp.bfloat16)] * count,
            scratch_shapes=[
                pltpu.VMEM((sides, pieces, size, size), jnp.bfloat16),
                pltpu.VMEM(*held_shape),
                pltpu.SemaphoreType.DMA((sides, flips)),
            ],
            compiler_params=small,
            cost_estimate=pl.CostEstimate(
                flops=2 * count * rows * size * (width + 4 * size),
                bytes_accessed=2 * (count * rows * width + width * size),
                transcendentals=count * rows * 4 * size,
            ),
            name="query",
        )(places, *token_sets, own, query_near, *parts[head], *memory[head], before[head])

    returned = [[] for _ in SIDES]
    for head in range(heads):
        if head < heads - 1:
            attended = query(head, tuple(range(sides)))
        else:
            away = query(head, tuple(range(1, sides)))
            attended = [*query(head, (0,), away[0]), *away]
        returned[0].append(attended[0])
        returned[1].append(xor_permute(attended[1], mesh, "ctx", 1))
        returned[2].append(xor_permute(attended[2], mesh, "groups", 1))
        returned[3].append(lax.ppermute(attended[3], ("groups", "ctx"), both))

    flat = [piece for side in returned for piece in side]
    return pl.pallas_call(
        functools.partial(merge_kernel, heads, size),
        in_specs=[SCALARS] + [VMEM] * len(flat),
        out_specs=VMEM,
        out_shape=jax.ShapeDtypeStruct((rows, heads_here * size), jnp.bfloat16),
        compiler_params=pltpu.CompilerParams(vmem_limit_bytes=8 << 20),
        name="merge",
    )(places, *flat)


def spreads(mesh, tokens, query_weight, key_weight, value_weight, log_decay):
    sizes = tuple(mesh.shape[axis] for axis in ("groups", "ctx", "fsdp", "head"))
    if sizes != (2, 4, 2, 2):
        return False
    heads_here = log_decay.shape[0]
    depth = query_weight.shape[0]
    size = query_weight.shape[1] // heads_here
    return (
        heads_here % 4 == 0
        and size == PIECE
        and depth % 128 == 0
        and depth * 4 == tokens.shape[1]
        and tokens.shape[0] % PIECE == 0
        and tokens.shape[0] <= 512
    )


def local_body(mesh, *arrays):
    if spreads(mesh, *arrays):
        return spread_body(mesh, *arrays)
    return body(*arrays)


def solution(mesh):
    return jax.shard_map(
        functools.partial(local_body, mesh),
        mesh=mesh,
        in_specs=(
            P(("groups", "ctx"), None),
            P("ctx", ("fsdp", "head")),
            P("ctx", ("fsdp", "head")),
            P("ctx", ("fsdp", "head")),
            P(("fsdp", "head"), ("groups", "ctx")),
        ),
        out_specs=P(("groups", "ctx"), ("fsdp", "head")),
        check_vma=False,
    )
```

```python
import functools
import jax
import jax.numpy as jnp
from jax import lax
from jax.experimental import pallas as pl
from jax.experimental.pallas import tpu as pltpu
from jax.sharding import PartitionSpec as P

EPSILON = 1e-06


def prefix(shard, axis, join, neutral):
    place = lax.axis_index(axis)
    gathered = jax.tree.map(
        lambda a, kind: lax.all_gather(a.astype(kind), axis), shard, (jnp.bfloat16, jnp.bfloat16)
    )
    state = jax.tree.map(lambda a, e: jnp.zeros_like(a) + jnp.asarray(e, a.dtype), shard, neutral)

    def one(turn, state):
        return join(
            state,
            jax.tree.map(
                lambda a, own: lax.dynamic_index_in_dim(a, turn, 0, False).astype(own.dtype),
                gathered,
                shard,
            ),
        )

    return lax.fori_loop(0, place, one, state)


def row_folder(tokens):

    def accumulate(running, portions, offset):
        return tuple(
            (jnp.dot(tokens, portion, preferred_element_type=jnp.float32) for portion in portions)
        )

    return accumulate


def combine_states(earlier, later):
    return (earlier[0] + later[0], jnp.exp(later[0])[:, None, None] * earlier[1] + later[1])


def local_summary(key_rows, value_rows, cumulative):
    heads_here, row_count = cumulative.shape
    head_size = key_rows.shape[1] // heads_here
    to_end = jnp.exp(cumulative[:, -1:] - cumulative)
    scaled = (
        key_rows.reshape(row_count, heads_here, head_size).astype(jnp.float32)
        * to_end.T[:, :, None]
    ).astype(jnp.bfloat16)
    valueset = value_rows.reshape(row_count, heads_here, head_size)
    return jnp.einsum("khd,khe->hde", scaled, valueset, preferred_element_type=jnp.float32)


def carried(total_decay, own_state):
    identity = (jnp.zeros_like(total_decay), jnp.zeros_like(own_state))
    return prefix((total_decay, own_state), "ctx", combine_states, identity)


def attend(query_rows, key_rows, value_rows, cumulative, incoming):
    heads_here, row_count = cumulative.shape
    head_size = query_rows.shape[1] // heads_here
    block_rows = min(row_count, 512)
    queries = query_rows.reshape(row_count, heads_here, head_size)
    keyset = key_rows.reshape(row_count, heads_here, head_size)
    valueset = value_rows.reshape(row_count, heads_here, head_size)
    incoming_bf = incoming.astype(jnp.bfloat16)
    key_index = jnp.arange(row_count)

    def one_block(block_index):
        first_row = block_index * block_rows
        query_index = first_row + jnp.arange(block_rows)
        scores = jnp.einsum("qhd,khd->hqk", queries, keyset, preferred_element_type=jnp.float32)
        causal = key_index[None, :] <= query_index[:, None]
        decay_gaps = jnp.where(
            causal[None], cumulative[:, :, None] - cumulative[:, None, :], -jnp.inf
        )
        weights = (scores * jnp.exp(decay_gaps)).astype(jnp.bfloat16)
        within_part = jnp.einsum(
            "hqk,khe->qhe", weights, valueset, preferred_element_type=jnp.float32
        )
        carried_part = (
            jnp.einsum("qhd,hde->qhe", queries, incoming_bf, preferred_element_type=jnp.float32)
            * jnp.exp(cumulative).T[:, :, None]
        )
        raw_out = within_part + carried_part
        inverse_rms = lax.rsqrt(jnp.mean(raw_out * raw_out, axis=-1, keepdims=True) + EPSILON)
        return (raw_out * inverse_rms).astype(jnp.bfloat16)

    blocks = lax.map(one_block, jnp.arange(row_count // block_rows))
    return blocks.reshape(row_count, heads_here * head_size)


def body(tokens, query_weight, key_weight, value_weight, log_decay):
    row_count = tokens.shape[0]
    zero_rows = jnp.zeros((row_count, query_weight.shape[1]), jnp.float32)
    accumulate = row_folder(tokens)
    cumulative = jnp.cumsum(log_decay, axis=1)
    total_decay = cumulative[:, -1]
    query_sum, key_sum, value_sum = accumulate(
        (zero_rows, zero_rows, zero_rows),
        (
            lax.all_gather(query_weight, "ctx", axis=0, tiled=True),
            lax.all_gather(key_weight, "ctx", axis=0, tiled=True),
            lax.all_gather(value_weight, "ctx", axis=0, tiled=True),
        ),
        jnp.int32(0),
    )
    query_rows = jax.nn.silu(query_sum).astype(jnp.bfloat16)
    key_rows = jax.nn.silu(key_sum).astype(jnp.bfloat16)
    value_rows = value_sum.astype(jnp.bfloat16)
    incoming = carried(total_decay, local_summary(key_rows, value_rows, cumulative))[1]
    return attend(query_rows, key_rows, value_rows, cumulative, incoming)


SIDES = ("own", "ctx", "groups", "both")
PIECE = 128
ANY = pl.BlockSpec(memory_space=pl.ANY)
VMEM = pl.BlockSpec(memory_space=pltpu.VMEM)
SCALARS = pl.BlockSpec(memory_space=pltpu.SMEM)


def xor_permute(array, mesh, axis, flip):
    return lax.ppermute(array, axis, [(at, at ^ flip) for at in range(mesh.shape[axis])])


def after(arrays, *earlier):
    return lax.optimization_barrier((*arrays, *earlier))[: len(arrays)]


def in_three(array):
    parts = []
    for _ in range(3):
        part = lax.reduce_precision(array, 8, 7)
        parts.append(part.astype(jnp.bfloat16))
        array = array - part
    return jnp.concatenate(parts, axis=0)


def silu(rows):
    return rows / (1.0 + jnp.exp(-rows))


def running_sum(rows):
    lane = lax.broadcasted_iota(jnp.int32, rows.shape, 1)
    shift = 1
    while shift < rows.shape[1]:
        rows += jnp.where(lane >= shift, pltpu.roll(rows, shift, 1), 0.0)
        shift *= 2
    return rows


def column_of(row):
    return jnp.transpose(jnp.broadcast_to(row, (PIECE, row.shape[1])))


def token_copies(places, token_refs, held, semaphores, chosen=range(len(SIDES))):
    turn, share = places[0], places[1] * 2 + places[2]
    own_ref, quarter_refs = token_refs[0], token_refs[1:]
    width = held.shape[3]

    def copy(source, side, flip):
        return pltpu.make_async_copy(source, held.at[side, flip], semaphores.at[side, flip])

    def start():
        for side in chosen:
            for flip in range(held.shape[1]):
                block = turn ^ flip
                if side == 0:
                    at = pl.multiple_of(block * width, width)
                    copy(own_ref.at[:, pl.ds(at, width)], side, flip).start()
                    continue
                for place, ref in enumerate(quarter_refs[4 * (side - 1) : 4 * side]):

                    @pl.when(block ^ share == place)
                    def _(ref=ref):
                        copy(ref.at[0 : held.shape[2], :], side, flip).start()

    def wait(side):
        for flip in range(held.shape[1]):
            copy(quarter_refs[0].at[0 : held.shape[2], :], side, flip).wait()

    return start, wait


def project(held, side, cut, weights):
    total = None
    for flip, weight in enumerate(weights):
        product = jnp.dot(held[side, flip, cut, :], weight, preferred_element_type=jnp.float32)
        total = product if total is None else total + product
    return total


def piece_rows(rows):
    return [slice(at, at + PIECE) for at in range(0, rows, PIECE)]


def staggered(items, *stages):
    carried = {}
    for turn in range(len(items) + len(stages) - 1):
        for depth in reversed(range(len(stages))):
            at = turn - depth
            if 0 <= at < len(items):
                carried[at] = stages[depth](items[at], carried.get(at))


def key_value_kernel(head_here, heads_all, size, flips, places, *refs):
    heads = 1
    sides = len(SIDES)
    token_refs, refs = refs[:13], refs[13:]
    tail_ref, refs = refs[0], refs[1:]
    source_ref, key_ref, value_ref, state_ref, sum_ref, fade_ref, mask_ref, pair_ref, held = refs[:9]
    weight_ref, decay_ref, end_ref, tails, semaphores, weight_semaphores, tail_semaphores = refs[9:]
    tail_rows = pl.ds(held.shape[2], tails.shape[1])
    tail_loads = [
        pltpu.make_async_copy(source, tails.at[side], tail_semaphores.at[side])
        for side, source in enumerate([tail_ref, *(ref.at[tail_rows, :] for ref in token_refs[1::4])])
    ]
    for load in tail_loads:
        load.start()
    columns = pl.ds(2 * head_here * size, 2 * size)
    loads = [
        pltpu.make_async_copy(
            source_ref.at[places[0] ^ flip, :, columns], weight_ref.at[flip], weight_semaphores.at[flip]
        )
        for flip in range(flips)
    ]
    for load in loads:
        load.start()
    start, wait = token_copies(places, token_refs, held, semaphores)
    start()
    odd = places[0] % 2 == 1
    causal = lax.broadcasted_iota(jnp.int32, (PIECE, PIECE), 1) <= lax.broadcasted_iota(
        jnp.int32, (PIECE, PIECE), 0
    )
    cuts = piece_rows(key_ref.shape[1])
    for load in loads:
        load.wait()

    def decays(side):
        tail_loads[side].wait()
        part = tails[side].astype(jnp.float32)
        count = part.shape[0] // 3
        log_decay = part[:count] + (part[count : 2 * count] + part[2 * count :])
        decay_ref[...] = running_sum(log_decay[:, : sum_ref.shape[2]])
        for head in range(heads):
            row = decay_ref[pl.ds(places[3] * heads_all + head_here, 1), :]
            sum_ref[side, head : head + 1, :] = row
            column = column_of(row)
            begin = jnp.zeros_like(column[:1])
            for cut in cuts:
                end = column[cut.stop - 1 : cut.stop, :]
                end_ref[head, side, cut, :] = jnp.exp(end - column[cut])
                fade_ref[head, side, cut, :] = jnp.exp(column[cut] - begin)
                gaps = jnp.where(causal, column[cut] - row[:, cut], -jnp.inf)
                mask_ref[head, side, cut, :] = jnp.exp(gaps)
                begin = end

    def first(item, _):
        side, head, piece = item
        if piece == 0:
            wait(side)
            decays(side)
        at = slice(2 * head * size, 2 * (head + 1) * size)
        return project(held, side, cuts[piece], [weight_ref[flip, :, at] for flip in range(flips)])

    def second(item, both):
        side, head, piece = item
        cut, to = cuts[piece], slice(head * size, (head + 1) * size)
        key = silu(both[:, :size]).astype(jnp.bfloat16)
        value = both[:, size:].astype(jnp.bfloat16)
        key_ref[side, cut, to] = key
        value_ref[side, cut, to] = value
        scaled = (key.astype(jnp.float32) * end_ref[head, side, cut, :]).astype(jnp.bfloat16)
        return scaled, value

    def third(item, pair):
        side, head, piece = item
        state = lax.dot_general(
            pair[0], pair[1], (((0,), (0,)), ((), ())), preferred_element_type=jnp.float32
        )
        if piece:
            sums, cut = sum_ref[side, head : head + 1, :], cuts[piece]
            fade = sums[:, cut.stop - 1 : cut.stop] - sums[:, cut.start - 1 : cut.start]
            state += jnp.exp(fade) * state_ref[head, side, piece - 1]
        state_ref[head, side, piece] = state

    staggered(
        [(side, head, piece) for side in range(sides) for head in range(heads) for piece in range(len(cuts))],
        first,
        second,
        third,
    )
    last = len(cuts) - 1
    end = sum_ref.shape[2] - 1
    for head in range(heads):
        for pair in range(2):
            own, other = state_ref[head, 2 * pair, last], state_ref[head, 2 * pair + 1, last]
            own_total = sum_ref[2 * pair, head : head + 1, end:]
            other_total = sum_ref[2 * pair + 1, head : head + 1, end:]
            total = jnp.where(odd, own_total, other_total)
            first, second = jnp.where(odd, other, own), jnp.where(odd, own, other)
            pair_ref[head, pair] = (jnp.exp(total) * first + second).astype(jnp.bfloat16)


def query_kernel(chosen, head, columns, flips, places, *refs):
    token_refs, refs = refs[:13], refs[13:]
    weight_refs, refs = refs[:flips], refs[flips:]
    key_ref, value_ref, state_ref, sum_ref, fade_ref, mask_ref, before_ref = refs[:7]
    out_refs, (incoming_ref, held, semaphores) = refs[7:-3], refs[-3:]
    out_refs = dict(zip(chosen, out_refs))
    start, wait = token_copies(places, token_refs, held, semaphores, chosen)
    start()
    odd = places[0] % 2 == 1
    cuts = piece_rows(key_ref.shape[1])
    last = len(cuts) - 1
    end = sum_ref.shape[2] - 1
    at = slice(head * PIECE, (head + 1) * PIECE)
    weights = [ref[:, columns] if flip == 1 else ref[...] for flip, ref in enumerate(weight_refs)]
    for side in chosen:
        partner = side ^ 1
        before = before_ref[head, side // 2].astype(jnp.float32)
        total = sum_ref[partner, head : head + 1, end:]
        later = jnp.exp(total) * before + state_ref[head, partner, last]
        second = odd if side % 2 == 0 else jnp.logical_not(odd)
        incoming = jnp.where(second, later, before)
        for piece, cut in enumerate(cuts):
            state = incoming
            if piece:
                sofar = jnp.exp(sum_ref[side, head : head + 1, cut.start - 1 : cut.start])
                state = state_ref[head, side, piece - 1] + sofar * incoming
            incoming_ref[side, piece] = state.astype(jnp.bfloat16)

    def first(item, _):
        side, piece = item
        if piece == 0:
            wait(side)
        return silu(project(held, side, cuts[piece], weights)).astype(jnp.bfloat16)

    def second(item, query):
        side, cut = item[0], cuts[item[1]]
        scores = lax.dot_general(
            query, key_ref[side, cut, at], (((1,), (1,)), ((), ())), preferred_element_type=jnp.float32
        )
        raw = jnp.dot(query, incoming_ref[side, item[1]], preferred_element_type=jnp.float32)
        return (scores * mask_ref[head, side, cut, :]).astype(jnp.bfloat16), raw * fade_ref[head, side, cut, :]

    def third(item, pair):
        side, cut = item[0], cuts[item[1]]
        return pair[1] + jnp.dot(pair[0], value_ref[side, cut, at], preferred_element_type=jnp.float32)

    def fourth(item, raw):
        side, cut = item[0], cuts[item[1]]
        scale = lax.rsqrt(jnp.mean(raw * raw, axis=1, keepdims=True) + EPSILON)
        out_refs[side][cut, :] = (raw * scale).astype(jnp.bfloat16)

    staggered(
        [(side, piece) for side in chosen for piece in range(len(cuts))], first, second, third, fourth
    )


def merge_kernel(heads, size, places, *refs):
    pieces, out_ref = refs[:-1], refs[-1]
    for side in range(len(SIDES)):
        for head in range(heads):
            at = pl.multiple_of(((places[3] ^ side) * heads + head) * size, size)
            out_ref[:, pl.ds(at, size)] = pieces[side * heads + head][...]


def pack_kernel(heads, size, places, *refs):
    out_ref = refs[4]
    for flip in range(out_ref.shape[0]):
        key_ref, value_ref = refs[2 * (flip % 2) : 2 * (flip % 2) + 2]
        for head in range(heads):
            at, to = head * size, 2 * head * size
            out_ref[places[0] ^ flip, :, to : to + size] = key_ref[:, at : at + size]
            out_ref[places[0] ^ flip, :, to + size : to + 2 * size] = value_ref[:, at : at + size]


def spread_body(mesh, tokens, query_weight, key_weight, value_weight, log_decay):
    rows, width = tokens.shape
    depth = query_weight.shape[0]
    heads_here = log_decay.shape[0]
    size = query_weight.shape[1] // heads_here
    flips = mesh.shape["ctx"]
    heads = heads_here // 4
    sides = len(SIDES)
    group, turn = lax.axis_index("groups"), lax.axis_index("ctx")
    plane, core = lax.axis_index("fsdp"), lax.axis_index("head")
    mine = group * 2 + turn % 2
    places = jnp.stack([turn, core, plane, mine]).astype(jnp.int32)
    both = [
        (at, (at // flips ^ 1) * flips + (at % flips ^ 1)) for at in range(mesh.shape["groups"] * flips)
    ]

    share = core * 2 + plane
    quarter = lax.dynamic_slice(tokens, (0, share * depth), (rows, depth))
    tail = jnp.pad(in_three(log_decay), ((0, 0), (0, depth - rows)))
    quarter = jnp.concatenate([quarter, tail], axis=0)

    steps = 2
    block = (depth // steps, heads * size)
    owners = pl.BlockSpec(block, lambda step, places: (step, places[3]))
    partners = pl.BlockSpec(block, lambda step, places: (step, places[3] ^ 1))
    packed_shape = (flips, depth, 2 * heads * size)
    packed = pl.pallas_call(
        functools.partial(pack_kernel, heads, size),
        grid_spec=pltpu.PrefetchScalarGridSpec(
            num_scalar_prefetch=1,
            grid=(steps,),
            in_specs=[owners, owners, partners, partners],
            out_specs=pl.BlockSpec((flips, depth // steps, 2 * heads * size), lambda step, places: (0, step, 0)),
        ),
        out_shape=jax.ShapeDtypeStruct(packed_shape, jnp.bfloat16),
        cost_estimate=pl.CostEstimate(flops=0, bytes_accessed=32 * depth * heads * size, transcendentals=0),
        name="pack",
    )(places, key_weight, value_weight, key_weight, value_weight)

    key_value = lax.all_to_all(packed, "ctx", 0, 0)

    from_ctx = xor_permute(quarter, mesh, "ctx", 1)
    from_groups = xor_permute(quarter, mesh, "groups", 1)
    ctx_core = xor_permute(from_ctx, mesh, "head", 1)
    (from_ctx,) = after((from_ctx,), ctx_core, from_groups)
    ctx_plane = xor_permute(from_ctx, mesh, "fsdp", 1)
    from_both = xor_permute(from_ctx, mesh, "groups", 1)
    beside = after((tokens,), from_ctx)[0]
    beside = lax.dynamic_slice(beside, (0, (share ^ 1) * depth), (rows, depth))
    groups_plane = xor_permute(beside, mesh, "groups", 1)
    both_core = xor_permute(from_both, mesh, "head", 1)
    (from_both,) = after((from_both,), both_core, ctx_plane)
    both_plane = xor_permute(from_both, mesh, "fsdp", 1)

    token_sets = [tokens]
    token_sets += [from_ctx, ctx_plane, ctx_core, xor_permute(ctx_plane, mesh, "head", 1)]
    for array in (from_groups, groups_plane):
        token_sets.append(array)
    token_sets += [xor_permute(array, mesh, "head", 1) for array in (from_groups, groups_plane)]
    token_sets += [from_both, both_plane, both_core, xor_permute(both_plane, mesh, "head", 1)]
    def query_block(owner, head, count):
        return lax.dynamic_slice(query_weight, (0, (owner * heads + head) * size), (depth, count * size))

    query_own = [query_block(mine, head, 1) for head in range(heads)]
    query_sent = [query_block(mine ^ 1, head, 1) for head in range(heads)]
    near_block, own, other = after(
        (query_block(mine ^ 1, 0, heads), query_own[0], query_sent[0]), from_both
    )
    query_near = xor_permute(near_block, mesh, "ctx", 1)
    parts = [
        [xor_permute(other if flip % 2 else own, mesh, "ctx", flip) for flip in range(2, flips)]
    ]

    large, small = (pltpu.CompilerParams(vmem_limit_bytes=size << 20) for size in (38, 24))
    pieces = rows // PIECE
    column_shape = (sides, rows, size)
    shapes = [
        (column_shape, jnp.bfloat16),
        (column_shape, jnp.bfloat16),
        ((1, sides, pieces, size, size), jnp.float32),
        ((sides, 1, rows), jnp.float32),
        ((1, sides, rows, size), jnp.float32),
        ((1, sides, rows, size), jnp.float32),
        ((1, 2, size, size), jnp.bfloat16),
    ]
    held_shape = ((sides, flips, rows, depth), jnp.bfloat16)
    memory, before = [], []
    for head in range(heads):
        results = pl.pallas_call(
            functools.partial(key_value_kernel, head, heads, size, flips),
            in_specs=[SCALARS] + [ANY] * (len(token_sets) + 2),
            out_specs=[VMEM] * len(shapes),
            scratch_shapes=[
                pltpu.VMEM(*held_shape),
                pltpu.VMEM((flips, depth, 2 * size), jnp.bfloat16),
                pltpu.VMEM(log_decay.shape, jnp.float32),
                pltpu.VMEM((1, sides, rows, size), jnp.float32),
                pltpu.VMEM((sides, *tail.shape), jnp.bfloat16),
                pltpu.SemaphoreType.DMA((sides, flips)),
                pltpu.SemaphoreType.DMA((flips,)),
                pltpu.SemaphoreType.DMA((sides,)),
            ],
            out_shape=[jax.ShapeDtypeStruct(*shape) for shape in shapes],
            compiler_params=large,
            cost_estimate=pl.CostEstimate(
                flops=2 * sides * rows * width * 2 * size,
                bytes_accessed=2 * (sides * rows * width + width * 2 * size),
                transcendentals=sides * rows * 2 * size,
            ),
            name="key_value",
        )(places, *token_sets, tail, key_value)
        memory.append(results[:6])
        pair_state = results[6]
        before.append(lax.ppermute(pair_state, "ctx", [(at, at + 2) for at in range(flips - 2)]))
        if head + 1 < heads:
            own, other = after((query_own[head + 1], query_sent[head + 1]), pair_state, query_near)
            parts.append(
                [xor_permute(other if flip % 2 else own, mesh, "ctx", flip) for flip in range(2, flips)]
            )

    def query(head, chosen, *gate):
        own = after((query_own[head],), *gate)[0] if gate else query_own[head]
        count = len(chosen)
        return pl.pallas_call(
            functools.partial(query_kernel, chosen, 0, slice(head * size, (head + 1) * size), flips),
            in_specs=[SCALARS] + [ANY] * len(token_sets) + [VMEM] * (flips + 7),
            out_specs=[VMEM] * count,
            out_shape=[jax.ShapeDtypeStruct((rows, size), jnp.bfloat16)] * count,
            scratch_shapes=[
                pltpu.VMEM((sides, pieces, size, size), jnp.bfloat16),
                pltpu.VMEM(*held_shape),
                pltpu.SemaphoreType.DMA((sides, flips)),
            ],
            compiler_params=small,
            cost_estimate=pl.CostEstimate(
                flops=2 * count * rows * size * (width + 4 * size),
                bytes_accessed=2 * (count * rows * width + width * size),
                transcendentals=count * rows * 4 * size,
            ),
            name="query",
        )(places, *token_sets, own, query_near, *parts[head], *memory[head], before[head])

    returned = [[] for _ in SIDES]
    for head in range(heads):
        if head < heads - 1:
            attended = query(head, tuple(range(sides)))
        else:
            away = query(head, tuple(range(1, sides)))
            attended = [*query(head, (0,), away[0]), *away]
        returned[0].append(attended[0])
        returned[1].append(xor_permute(attended[1], mesh, "ctx", 1))
        returned[2].append(xor_permute(attended[2], mesh, "groups", 1))
        returned[3].append(lax.ppermute(attended[3], ("groups", "ctx"), both))

    flat = [piece for side in returned for piece in side]
    return pl.pallas_call(
        functools.partial(merge_kernel, heads, size),
        in_specs=[SCALARS] + [VMEM] * len(flat),
        out_specs=VMEM,
        out_shape=jax.ShapeDtypeStruct((rows, heads_here * size), jnp.bfloat16),
        compiler_params=pltpu.CompilerParams(vmem_limit_bytes=8 << 20),
        name="merge",
    )(places, *flat)


def spreads(mesh, tokens, query_weight, key_weight, value_weight, log_decay):
    sizes = tuple(mesh.shape[axis] for axis in ("groups", "ctx", "fsdp", "head"))
    if sizes != (2, 4, 2, 2):
        return False
    heads_here = log_decay.shape[0]
    depth = query_weight.shape[0]
    size = query_weight.shape[1] // heads_here
    return (
        heads_here % 4 == 0
        and size == PIECE
        and depth % 128 == 0
        and depth * 4 == tokens.shape[1]
        and tokens.shape[0] % PIECE == 0
        and tokens.shape[0] <= 512
    )


def local_body(mesh, *arrays):
    if spreads(mesh, *arrays):
        return spread_body(mesh, *arrays)
    return body(*arrays)


def solution(mesh):
    return jax.shard_map(
        functools.partial(local_body, mesh),
        mesh=mesh,
        in_specs=(
            P(("groups", "ctx"), None),
            P("ctx", ("fsdp", "head")),
            P("ctx", ("fsdp", "head")),
            P("ctx", ("fsdp", "head")),
            P(("fsdp", "head"), ("groups", "ctx")),
        ),
        out_specs=P(("groups", "ctx"), ("fsdp", "head")),
        check_vma=False,
    )
```
